256 devices in a mesh: dp: 8 (over y_hi, x), frame: 32 (over y_lo, z, core).
Axes of the slice: x: 4, y: 4 (y_hi: 2, y_lo: 2; y = y_hi * 2 + y_lo), z: 8, core: 2. Of those that a mesh axis runs over, the one named last changes fastest.
Arguments:
- video: bfloat16 [8, 128, 8, 64, 256], P('dp', 'frame'), may hold values from -6 to 6
- saved: bfloat16 [8, 128, 8, 64, 256], P('dp', 'frame'), may hold values from -6 to 6
- grad_out: bfloat16 [8, 128, 8, 64, 256], P('dp', 'frame'), may hold values from -6 to 6
- spatial_w: bfloat16 [2304, 256], replicated, may hold values from -0.125 to 0.125
- temporal_w: bfloat16 [768, 256], replicated, may hold values from -0.21875 to 0.21875
Outputs:
- grad_video: bfloat16 [8, 128, 8, 64, 256], P('dp', 'frame')
- grad_spatial: float32 [2304, 256], P('frame', 'dp')
- grad_temporal: float32 [768, 256], P('frame', 'dp')
The draws below stay inside these ranges and needn't reach their ends.
All inputs are finite; a program needn't handle non-finite values.
Results may differ from the reference program's by a relative error of at most 0.0049.
Values may be sent and summed in bfloat16 or wider, within the bound.
No kernel may reach another device: no remote copies, remote signals or barrier semaphores. Data moves between devices by JAX's collectives and lax.ppermute only.
A program may use at most 64 MiB of HBM per device.

```python
import math
import jax
import jax.numpy as jnp
from jax import lax

C = 256
KS = 9
KT = 3
HGT = 8
WID = 64
CLIPS = 8
FRAMES = 128


def level_of(rng, extent, split, low, largest):
    def one(dim, blocks):
        steps = jax.random.uniform(jax.random.fold_in(jax.random.fold_in(rng, 6), dim), (blocks,), jnp.float32, low / len(split), largest / len(split))
        return jnp.repeat(jnp.exp(steps), extent[dim] // blocks).reshape((-1,) + (1,) * (len(extent) - dim - 1))

    level = one(*split[0])
    for cut in split[1:]:
        level = level * one(*cut)
    return level


def bell_draw(rng, dims, deviation, bound, cuts=(), kind=jnp.bfloat16):
    drawn = jax.random.normal(rng, dims, jnp.float32) * deviation
    if len(cuts) > 0:
        drawn = level_of(rng, dims, cuts, -0.22, 0.18) * drawn
    return jnp.clip(drawn, min=-bound, max=bound).astype(kind)


def setup_inputs(seed: int = 0) -> dict:
    key_of = jax.random.split(jax.random.key(seed), 6)
    return {
        "video": bell_draw(key_of[0], (CLIPS, FRAMES, HGT, WID, C), 1.0, 6.0, ((0, 8), (1, 32))),
        "saved": bell_draw(key_of[1], (CLIPS, FRAMES, HGT, WID, C), 1.0, 6.0, ((0, 8), (1, 32))),
        "grad_out": bell_draw(key_of[2], (CLIPS, FRAMES, HGT, WID, C), 1.0, 6.0, ((0, 8), (1, 32))),
        "spatial_w": bell_draw(key_of[3], (KS * C, C), (KS * C) ** -0.5, 0.125),
        "temporal_w": bell_draw(key_of[4], (KT * C, C), (KT * C) ** -0.5, 0.21875),
    }


def shifted(source, row_off, col_off):
    height = source.shape[1]
    width = source.shape[2]
    padded = jnp.pad(source, ((0, 0), (1, 1), (1, 1), (0, 0)))
    return padded[:, 1 + row_off:1 + row_off + height, 1 + col_off:1 + col_off + width, :]

def temporal_back(grad_ext, saved_ext, frames, temporal_w, channels):
    lag_count = temporal_w.shape[0] // channels
    grad_now = grad_ext[:frames].reshape(-1, channels)
    hidden = jnp.zeros((grad_now.shape[0], channels), jnp.float32)
    blocks = []
    for lag in range(lag_count):
        weight_block = temporal_w[lag * channels:(lag + 1) * channels]
        later = grad_ext[lag:lag + frames].reshape(-1, channels)
        hidden = hidden + lax.dot_general(later, weight_block, (((1,), (1,)), ((), ())), preferred_element_type=jnp.float32)
        earlier = saved_ext[lag_count - 1 - lag:lag_count - 1 - lag + frames].reshape(-1, channels)
        blocks.append(lax.dot_general(earlier, grad_now, (((0,), (0,)), ((), ())), preferred_element_type=jnp.float32))
    return (hidden.astype(jnp.bfloat16), jnp.concatenate(blocks, axis=0))

def spatial_back(video_clip, grad_hidden, spatial_w, channels):
    grad_flat = grad_hidden.reshape(-1, channels)
    result = jnp.zeros(grad_flat.shape, jnp.float32)
    blocks = []
    for row_off in (-1, 0, 1):
        for col_off in (-1, 0, 1):
            tap_index = (row_off + 1) * 3 + (col_off + 1)
            weight_block = spatial_w[tap_index * channels:(tap_index + 1) * channels]
            moved = shifted(grad_hidden, -row_off, -col_off).reshape(-1, channels)
            result = result + lax.dot_general(moved, weight_block, (((1,), (1,)), ((), ())), preferred_element_type=jnp.float32)
            patch = shifted(video_clip, row_off, col_off).reshape(-1, channels)
            blocks.append(lax.dot_general(patch, grad_flat, (((0,), (0,)), ((), ())), preferred_element_type=jnp.float32))
    return (result.astype(jnp.bfloat16).reshape(grad_hidden.shape), jnp.concatenate(blocks, axis=0))

def reference(video, saved, grad_out, spatial_w, temporal_w):

    def one_clip(items):
        video_clip, saved_clip, grad_clip = items
        rim_zeros = jnp.zeros((KT - 1,) + grad_clip.shape[1:], jnp.bfloat16)
        grad_ext = jnp.concatenate([grad_clip, rim_zeros], axis=0)
        saved_ext = jnp.concatenate([rim_zeros, saved_clip], axis=0)
        hidden, wt_part = temporal_back(grad_ext, saved_ext, FRAMES, temporal_w, C)
        hidden = hidden.reshape(grad_clip.shape)
        grad_clip_in, ws_part = spatial_back(video_clip, hidden, spatial_w, C)
        return (grad_clip_in, ws_part, wt_part)
    grad_video, ws_parts, wt_parts = lax.map(one_clip, (video, saved, grad_out))
    factor = 1.0 / math.sqrt(float(CLIPS * FRAMES * HGT * WID))
    return (grad_video, lax.optimization_barrier(jnp.sum(ws_parts, axis=0)) * factor, lax.optimization_barrier(jnp.sum(wt_parts, axis=0)) * factor)
```

```python
import math

import jax
import jax.numpy as jnp
from jax import lax
from jax.experimental import pallas as pl
from jax.experimental.pallas import tpu as pltpu
from jax.sharding import PartitionSpec as P


C = 256
WID = 64
PIX = 512
WS = 9 * C
WT = 3 * C
F32 = jnp.float32
BF16 = jnp.bfloat16
VMEM_LIMIT = 40 * 1024 * 1024


def dot_t(a, b):
    return lax.dot_general(a, b, (((1,), (1,)), ((), ())), preferred_element_type=F32)


def dot_n(a, b):
    return lax.dot_general(a, b, (((1,), (0,)), ((), ())), preferred_element_type=F32)


def fill_shifted(hidden, shifted_ref, frame):
    column = lax.broadcasted_iota(jnp.int32, (PIX, C), 0) % WID
    zeros = jnp.zeros((WID, C), BF16)
    right = jnp.where(column == 0, 0.0, pltpu.roll(hidden, 1, 0))
    left = jnp.where(column == WID - 1, 0.0, pltpu.roll(hidden, PIX - 1, 0))
    for slot, value in ((0, left), (1, hidden), (2, right)):
        shifted_ref[slot, frame, 0:WID] = zeros
        shifted_ref[slot, frame, WID : WID + PIX] = value.astype(BF16)
        shifted_ref[slot, frame, WID + PIX : 2 * WID + PIX] = zeros


def tap_rows(tap):
    row_off = tap // 3 - 1
    slot = tap % 3
    return slot, WID - WID * row_off


def spatial(shifted_ref, video_ref, video_t_ref, ws_w_ref, gv_ref, emit):
    for frame in range(2):
        video_t_ref[:, frame * PIX : (frame + 1) * PIX] = video_ref[frame].T
    for frame in range(2):
        total = jnp.zeros((PIX, C), F32)
        for tap in range(9):
            slot, low = tap_rows(tap)
            total = total + dot_t(shifted_ref[slot, frame, low : low + PIX], ws_w_ref[tap * C : (tap + 1) * C])
        gv_ref[frame] = total.astype(BF16)
    for tap in range(9):
        slot, low = tap_rows(tap)
        rows = shifted_ref[slot, :, low : low + PIX].reshape(2 * PIX, C)
        emit(tap, dot_n(video_t_ref[...], rows))


def first_kernel(grad_ref, saved_ref, video_ref, ws_w_ref, wt_w_ref, gv_ref, acc_ref, shifted_ref, video_t_ref, saved_t_ref):
    for frame in range(4):
        saved_t_ref[:, frame * PIX : (frame + 1) * PIX] = saved_ref[frame].T
    for lag in range(3):
        rows = grad_ref[lag:4].reshape((4 - lag) * PIX, C)
        acc_ref[WS + lag * C : WS + (lag + 1) * C] = dot_n(saved_t_ref[:, : (4 - lag) * PIX], rows)
    for frame in range(2):
        hidden = jnp.zeros((PIX, C), F32)
        for lag in range(3):
            hidden = hidden + dot_t(grad_ref[frame + lag], wt_w_ref[lag * C : (lag + 1) * C])
        fill_shifted(hidden, shifted_ref, frame)

    def emit(tap, value):
        acc_ref[tap * C : (tap + 1) * C] = value

    spatial(shifted_ref, video_ref, video_t_ref, ws_w_ref, gv_ref, emit)


def pack(total_ref, first_row, quarter, out_ref, out_row):
    group = lax.broadcasted_iota(jnp.int32, (quarter, 128), 1) // 32
    for y_lo in range(2):
        for half in range(2):
            parts = [
                total_ref[pl.ds(first_row + (y_lo * 4 + j) * quarter, quarter), half * 128 : (half + 1) * 128]
                for j in range(4)
            ]
            for dq in range(4):
                value = parts[dq]
                for j in range(4):
                    if j != dq:
                        value = jnp.where(group == j, pltpu.roll(parts[j], ((j - dq) * 32) % 128, 1), value)
                out_ref[(half * 4 + dq) * 2 + y_lo, out_row : out_row + quarter] = value.astype(BF16)


def second_kernel(
    grad_ref, halo_ref, saved_ref, video_ref, ws_w_ref, wt_w_ref, acc_ref, gv_in_ref, gv_ref, out_ref,
    shifted_ref, video_t_ref, saved_t_ref, total_ref,
):
    del gv_in_ref
    frames = [grad_ref[0], grad_ref[1], halo_ref[0], halo_ref[1]]
    for frame in range(2):
        hidden = jnp.zeros((PIX, C), F32)
        for lag in range(3):
            hidden = hidden + dot_t(frames[frame + lag], wt_w_ref[lag * C : (lag + 1) * C])
        fill_shifted(hidden, shifted_ref, frame)
    for frame in range(2):
        saved_t_ref[:, frame * PIX : (frame + 1) * PIX] = saved_ref[frame].T
    total_ref[WS : WS + C] = acc_ref[WS : WS + C]
    total_ref[WS + C : WS + 2 * C] = acc_ref[WS + C : WS + 2 * C] + dot_n(saved_t_ref[:, PIX:], halo_ref[0])
    total_ref[WS + 2 * C :] = acc_ref[WS + 2 * C :] + dot_n(saved_t_ref[...], halo_ref[...].reshape(2 * PIX, C))

    def emit(tap, value):
        total_ref[tap * C : (tap + 1) * C] = acc_ref[tap * C : (tap + 1) * C] + value

    spatial(shifted_ref, video_ref, video_t_ref, ws_w_ref, gv_ref, emit)
    pack(total_ref, 0, WS // 8, out_ref, 0)
    pack(total_ref, WS, WT // 8, out_ref, WS // 8)


def middle_kernel(in_ref, out_ref, sum_ref):
    total = in_ref[0].astype(F32)
    for source in range(1, 16):
        total = total + in_ref[source].astype(F32)
    sum_ref[...] = total
    group = lax.broadcasted_iota(jnp.int32, (24, 128), 1) // 32
    for q in range(4):
        rows = [sum_ref[72 * q + 24 * g : 72 * q + 24 * (g + 1)] for g in range(3)]
        rows.append(sum_ref[288 + 24 * q : 288 + 24 * (q + 1)])
        for j in range(4):
            value = rows[j]
            for g in range(4):
                if g != j:
                    value = jnp.where(group == g, pltpu.roll(rows[g], ((g - j) * 32) % 128, 1), value)
            out_ref[(2 * j + q // 2) * 2 + q % 2] = value.astype(BF16)


def last_kernel(factor, in_ref, ws_ref, wt_ref):
    total = in_ref[0].astype(F32)
    for source in range(1, 16):
        total = total + in_ref[source].astype(F32)
    total = total * factor
    for g in range(3):
        ws_ref[24 * g : 24 * (g + 1), :] = total[:, 32 * g : 32 * (g + 1)]
    wt_ref[...] = total[:, 96:128]


def frames_spec(index, count=2):
    return pl.BlockSpec((count, PIX, C), lambda i: (index, 0, 0))


def whole(*shape):
    return pl.BlockSpec(shape, lambda i: (0,) * len(shape))


def run_first(grad, saved, video, ws_w, wt_w):
    return pl.pallas_call(
        first_kernel,
        grid=(1,),
        out_shape=(jax.ShapeDtypeStruct((4, PIX, C), BF16), jax.ShapeDtypeStruct((WS + WT, C), F32)),
        in_specs=[frames_spec(0, 4), frames_spec(0, 4), frames_spec(0), whole(WS, C), whole(WT, C)],
        out_specs=(frames_spec(0), whole(WS + WT, C)),
        scratch_shapes=[
            pltpu.VMEM((3, 2, PIX + 2 * WID, C), BF16),
            pltpu.VMEM((C, 2 * PIX), BF16),
            pltpu.VMEM((C, 4 * PIX), BF16),
        ],
        compiler_params=pltpu.CompilerParams(vmem_limit_bytes=VMEM_LIMIT),
        cost_estimate=pl.CostEstimate(flops=4_000_000_000, bytes_accessed=8_000_000, transcendentals=0),
        name="first",
    )(grad, saved, video, ws_w, wt_w)


def run_second(grad, halo, saved, video, ws_w, wt_w, acc, gv):
    return pl.pallas_call(
        second_kernel,
        grid=(1,),
        out_shape=(jax.ShapeDtypeStruct((4, PIX, C), BF16), jax.ShapeDtypeStruct((16, 384, 128), BF16)),
        in_specs=[
            frames_spec(1), frames_spec(0), frames_spec(1), frames_spec(1), whole(WS, C), whole(WT, C),
            whole(WS + WT, C), pl.BlockSpec(memory_space=pl.ANY),
        ],
        out_specs=(frames_spec(1), whole(16, 384, 128)),
        scratch_shapes=[
            pltpu.VMEM((3, 2, PIX + 2 * WID, C), BF16),
            pltpu.VMEM((C, 2 * PIX), BF16),
            pltpu.VMEM((C, 2 * PIX), BF16),
            pltpu.VMEM((WS + WT, C), F32),
        ],
        input_output_aliases={7: 0},
        compiler_params=pltpu.CompilerParams(vmem_limit_bytes=VMEM_LIMIT),
        cost_estimate=pl.CostEstimate(flops=3_000_000_000, bytes_accessed=9_000_000, transcendentals=0),
        name="second",
    )(grad, halo, saved, video, ws_w, wt_w, acc, gv)


def run_middle(received):
    return pl.pallas_call(
        middle_kernel,
        grid=(1,),
        out_shape=jax.ShapeDtypeStruct((16, 24, 128), BF16),
        in_specs=[whole(16, 384, 128)],
        out_specs=whole(16, 24, 128),
        scratch_shapes=[pltpu.VMEM((384, 128), F32)],
        compiler_params=pltpu.CompilerParams(vmem_limit_bytes=VMEM_LIMIT),
        name="middle",
    )(received)


def run_last(received, factor):
    def kernel(*refs):
        last_kernel(factor, *refs)

    return pl.pallas_call(
        kernel,
        grid=(1,),
        out_shape=(jax.ShapeDtypeStruct((72, 32), F32), jax.ShapeDtypeStruct((24, 32), F32)),
        in_specs=[whole(16, 24, 128)],
        out_specs=(whole(72, 32), whole(24, 32)),
        compiler_params=pltpu.CompilerParams(vmem_limit_bytes=VMEM_LIMIT),
        name="last",
    )(received)


def local(video, saved, grad_out, spatial_w, temporal_w):
    shape = grad_out.shape
    grad = grad_out.reshape(4, PIX, C)
    saved = saved.reshape(4, PIX, C)
    video = video.reshape(4, PIX, C)
    halo = lax.ppermute(grad[0:2], "frame", [(i, i - 1) for i in range(1, 32)])
    gv, acc = run_first(grad, saved, video, spatial_w, temporal_w)
    gv, packed = run_second(grad, halo, saved, video, spatial_w, temporal_w, acc, gv)
    planes = [[(d * 2 + y) * 16 + f for d in range(8) for y in range(2)] for f in range(16)]
    rows = lax.all_to_all(packed, ("dp", "frame"), 0, 0, tiled=True, axis_index_groups=planes)
    blocks = run_middle(rows)
    columns = [[y * 16 + f for f in range(16)] for y in range(2)]
    owned = lax.all_to_all(blocks, "frame", 0, 0, tiled=True, axis_index_groups=columns)
    factor = 1.0 / math.sqrt(float(8 * 128 * 8 * 64))
    grad_spatial, grad_temporal = run_last(owned, factor)
    return (gv.reshape(shape), grad_spatial, grad_temporal)


def solution(mesh):
    return jax.shard_map(
        local,
        mesh=mesh,
        in_specs=(
            P("dp", "frame", None, None, None),
            P("dp", "frame", None, None, None),
            P("dp", "frame", None, None, None),
            P(),
            P(),
        ),
        out_specs=(P("dp", "frame", None, None, None), P("frame", "dp"), P("frame", "dp")),
        check_vma=False,
    )
```

```python
import math

import jax
import jax.numpy as jnp
from jax import lax
from jax.experimental import pallas as pl
from jax.experimental.pallas import tpu as pltpu
from jax.sharding import PartitionSpec as P


C = 256
WID = 64
PIX = 512
WS = 9 * C
WT = 3 * C
F32 = jnp.float32
BF16 = jnp.bfloat16
VMEM_LIMIT = 40 * 1024 * 1024


def dot_t(a, b):
    return lax.dot_general(a, b, (((1,), (1,)), ((), ())), preferred_element_type=F32)


def dot_n(a, b):
    return lax.dot_general(a, b, (((1,), (0,)), ((), ())), preferred_element_type=F32)


def fill_shifted(hidden, shifted_ref, frame):
    column = lax.broadcasted_iota(jnp.int32, (PIX, C), 0) % WID
    zeros = jnp.zeros((WID, C), BF16)
    right = jnp.where(column == 0, 0.0, pltpu.roll(hidden, 1, 0))
    left = jnp.where(column == WID - 1, 0.0, pltpu.roll(hidden, PIX - 1, 0))
    for slot, value in ((0, left), (1, hidden), (2, right)):
        shifted_ref[slot, frame, 0:WID] = zeros
        shifted_ref[slot, frame, WID : WID + PIX] = value.astype(BF16)
        shifted_ref[slot, frame, WID + PIX : 2 * WID + PIX] = zeros


def tap_rows(tap):
    row_off = tap // 3 - 1
    slot = tap % 3
    return slot, WID - WID * row_off


def spatial(frames, shifted_ref, video_ref, video_t_ref, ws_w_ref, gv_ref, emit):
    for frame in range(frames):
        video_t_ref[:, frame * PIX : (frame + 1) * PIX] = video_ref[frame].T
    for frame in range(frames):
        total = jnp.zeros((PIX, C), F32)
        for tap in range(9):
            slot, low = tap_rows(tap)
            total = total + dot_t(shifted_ref[slot, frame, low : low + PIX], ws_w_ref[tap * C : (tap + 1) * C])
        gv_ref[frame] = total.astype(BF16)
    for tap in range(9):
        slot, low = tap_rows(tap)
        rows = shifted_ref[slot, :, low : low + PIX].reshape(frames * PIX, C)
        emit(tap, dot_n(video_t_ref[...], rows))


def hidden_of(frames, wt_w_ref):
    hidden = jnp.zeros((PIX, C), F32)
    for lag in range(3):
        hidden = hidden + dot_t(frames[lag], wt_w_ref[lag * C : (lag + 1) * C])
    return hidden


def first_kernel(
    grad_hbm, saved_hbm, video_hbm, ws_w_hbm, wt_w_hbm, gv_ref, acc_ref,
    grad_ref, saved_ref, video_ref, ws_w_ref, wt_w_ref, shifted_ref, video_t_ref, saved_t_ref, sems,
):
    sources = (saved_hbm, grad_hbm, wt_w_hbm, video_hbm.at[0:2], ws_w_hbm)
    targets = (saved_ref, grad_ref, wt_w_ref, video_ref, ws_w_ref)
    copies = [pltpu.make_async_copy(a, b, sems.at[i]) for i, (a, b) in enumerate(zip(sources, targets))]
    for copy in copies:
        copy.start()
    copies[0].wait()
    for frame in range(4):
        saved_t_ref[:, frame * PIX : (frame + 1) * PIX] = saved_ref[frame].T
    copies[1].wait()
    for lag in range(3):
        rows = grad_ref[lag:4].reshape((4 - lag) * PIX, C)
        acc_ref[WS + lag * C : WS + (lag + 1) * C] = dot_n(saved_t_ref[:, : (4 - lag) * PIX], rows)
    copies[2].wait()
    for frame in range(2):
        fill_shifted(hidden_of([grad_ref[frame + lag] for lag in range(3)], wt_w_ref), shifted_ref, frame)
    copies[3].wait()
    copies[4].wait()

    def emit(tap, value):
        acc_ref[tap * C : (tap + 1) * C] = value

    spatial(2, shifted_ref, video_ref, video_t_ref, ws_w_ref, gv_ref, emit)


def third_frame_kernel(
    grad_ref, halo_ref, saved_ref, video_ref, ws_w_ref, wt_w_ref, acc_ref, gv_in_ref, gv_ref, out_ref,
    shifted_ref, video_t_ref,
):
    del gv_in_ref
    fill_shifted(hidden_of([grad_ref[0], grad_ref[1], halo_ref[0]], wt_w_ref), shifted_ref, 0)
    out_ref[WS : WS + C] = acc_ref[WS : WS + C]
    for lag in (1, 2):
        rows = slice(WS + lag * C, WS + (lag + 1) * C)
        out_ref[rows] = acc_ref[rows] + dot_n(saved_ref[2 - lag].T, halo_ref[0])

    def emit(tap, value):
        out_ref[tap * C : (tap + 1) * C] = acc_ref[tap * C : (tap + 1) * C] + value

    spatial(1, shifted_ref, video_ref, video_t_ref, ws_w_ref, gv_ref, emit)


def pack(total_ref, first_row, count, core, out_ref, out_row):
    group = lax.broadcasted_iota(jnp.int32, (count, 128), 1) // 32
    for y_lo in range(2):
        for z_low in range(2):
            for half in range(2):
                parts = []
                for j in range(4):
                    row = pl.multiple_of(first_row + (((y_lo * 8 + 2 * j + z_low) * 2) + core) * count, 8)
                    parts.append(total_ref[pl.ds(row, count), half * 128 : (half + 1) * 128])
                for dq in range(4):
                    value = parts[dq]
                    for j in range(4):
                        if j != dq:
                            value = jnp.where(group == j, pltpu.roll(parts[j], ((j - dq) * 32) % 128, 1), value)
                    low = out_row + z_low * count
                    out_ref[(half * 4 + dq) * 2 + y_lo, low : low + count] = value.astype(BF16)


def fourth_frame_kernel(
    core_ref, grad_ref, halo_a_ref, halo_b_ref, saved_ref, video_ref, ws_w_ref, wt_w_ref, acc_ref, gv_in_ref,
    gv_ref, send_ref, keep_ref, shifted_ref, video_t_ref, total_ref,
):
    del gv_in_ref
    fill_shifted(hidden_of([grad_ref[0], halo_a_ref[0], halo_b_ref[0]], wt_w_ref), shifted_ref, 0)
    total_ref[WS : WS + 2 * C] = acc_ref[WS : WS + 2 * C]
    total_ref[WS + 2 * C :] = acc_ref[WS + 2 * C :] + dot_n(saved_ref[0].T, halo_b_ref[0])

    def emit(tap, value):
        total_ref[tap * C : (tap + 1) * C] = acc_ref[tap * C : (tap + 1) * C] + value

    spatial(1, shifted_ref, video_ref, video_t_ref, ws_w_ref, gv_ref, emit)
    core = core_ref[0]
    for target, ref in ((1 - core, send_ref), (core, keep_ref)):
        pack(total_ref, 0, 72, target, ref, 0)
        pack(total_ref, WS, 24, target, ref, 144)


def middle_kernel(in_ref, out_ref, sum_ref):
    total = in_ref[0].astype(F32)
    for source in range(1, 16):
        total = total + in_ref[source].astype(F32)
    sum_ref[...] = total
    group = lax.broadcasted_iota(jnp.int32, (24, 128), 1) // 32
    for z_low in range(2):
        rows = [sum_ref[72 * z_low + 24 * g : 72 * z_low + 24 * (g + 1)] for g in range(3)]
        rows.append(sum_ref[144 + 24 * z_low : 144 + 24 * (z_low + 1)])
        for j in range(4):
            value = rows[j]
            for g in range(4):
                if g != j:
                    value = jnp.where(group == g, pltpu.roll(rows[g], ((g - j) * 32) % 128, 1), value)
            out_ref[2 * j + z_low] = value.astype(BF16)


def last_kernel(factor, in_ref, ws_ref, wt_ref):
    total = in_ref[0].astype(F32)
    for source in range(1, 8):
        total = total + in_ref[source].astype(F32)
    total = total * factor
    for g in range(3):
        ws_ref[:, 24 * g : 24 * (g + 1)] = total[:, 32 * g : 32 * (g + 1)].T
    wt_ref[...] = total[:, 96:128]


def frames_spec(index, count=2):
    return pl.BlockSpec((count, PIX, C), lambda i: (index, 0, 0))


def whole(*shape):
    return pl.BlockSpec(shape, lambda i: (0,) * len(shape))


def in_place():
    return pl.BlockSpec(memory_space=pltpu.MemorySpace.HBM)


def run_first(grad, saved, video, ws_w, wt_w):
    return pl.pallas_call(
        first_kernel,
        grid=(1,),
        out_shape=(jax.ShapeDtypeStruct((4, PIX, C), BF16), jax.ShapeDtypeStruct((WS + WT, C), F32)),
        in_specs=[in_place()] * 5,
        out_specs=(frames_spec(0), whole(WS + WT, C)),
        scratch_shapes=[
            pltpu.VMEM((4, PIX, C), BF16),
            pltpu.VMEM((4, PIX, C), BF16),
            pltpu.VMEM((2, PIX, C), BF16),
            pltpu.VMEM((WS, C), BF16),
            pltpu.VMEM((WT, C), BF16),
            pltpu.VMEM((3, 2, PIX + 2 * WID, C), BF16),
            pltpu.VMEM((C, 2 * PIX), BF16),
            pltpu.VMEM((C, 4 * PIX), BF16),
            pltpu.SemaphoreType.DMA((5,)),
        ],
        compiler_params=pltpu.CompilerParams(vmem_limit_bytes=VMEM_LIMIT),
        cost_estimate=pl.CostEstimate(flops=4_000_000_000, bytes_accessed=8_000_000, transcendentals=0),
        name="first",
    )(grad, saved, video, ws_w, wt_w)


def run_third(grad, halo, saved, video, ws_w, wt_w, acc, gv):
    return pl.pallas_call(
        third_frame_kernel,
        grid=(1,),
        out_shape=(jax.ShapeDtypeStruct((4, PIX, C), BF16), jax.ShapeDtypeStruct((WS + WT, C), F32)),
        in_specs=[
            frames_spec(1), frames_spec(0, 1), frames_spec(1), frames_spec(2, 1), whole(WS, C), whole(WT, C),
            whole(WS + WT, C), pl.BlockSpec(memory_space=pl.ANY),
        ],
        out_specs=(frames_spec(2, 1), whole(WS + WT, C)),
        scratch_shapes=[pltpu.VMEM((3, 1, PIX + 2 * WID, C), BF16), pltpu.VMEM((C, PIX), BF16)],
        input_output_aliases={7: 0},
        compiler_params=pltpu.CompilerParams(vmem_limit_bytes=VMEM_LIMIT),
        cost_estimate=pl.CostEstimate(flops=1_500_000_000, bytes_accessed=5_000_000, transcendentals=0),
        name="third_frame",
    )(grad, halo, saved, video, ws_w, wt_w, acc, gv)


def run_fourth(core, grad, halo_a, halo_b, saved, video, ws_w, wt_w, acc, gv):
    packed = jax.ShapeDtypeStruct((16, 192, 128), BF16)
    return pl.pallas_call(
        fourth_frame_kernel,
        grid=(1,),
        out_shape=(jax.ShapeDtypeStruct((4, PIX, C), BF16), packed, packed),
        in_specs=[
            pl.BlockSpec(memory_space=pltpu.MemorySpace.SMEM), frames_spec(3, 1), frames_spec(0, 1), frames_spec(0, 1),
            frames_spec(3, 1), frames_spec(3, 1), whole(WS, C), whole(WT, C), whole(WS + WT, C),
            pl.BlockSpec(memory_space=pl.ANY),
        ],
        out_specs=(frames_spec(3, 1), whole(16, 192, 128), whole(16, 192, 128)),
        scratch_shapes=[
            pltpu.VMEM((3, 1, PIX + 2 * WID, C), BF16),
            pltpu.VMEM((C, PIX), BF16),
            pltpu.VMEM((WS + WT, C), F32),
        ],
        input_output_aliases={9: 0},
        compiler_params=pltpu.CompilerParams(vmem_limit_bytes=VMEM_LIMIT),
        cost_estimate=pl.CostEstimate(flops=1_500_000_000, bytes_accessed=5_000_000, transcendentals=0),
        name="fourth_frame",
    )(core, grad, halo_a, halo_b, saved, video, ws_w, wt_w, acc, gv)


def run_middle(received):
    return pl.pallas_call(
        middle_kernel,
        grid=(1,),
        out_shape=jax.ShapeDtypeStruct((8, 24, 128), BF16),
        in_specs=[whole(16, 192, 128)],
        out_specs=whole(8, 24, 128),
        scratch_shapes=[pltpu.VMEM((192, 128), F32)],
        compiler_params=pltpu.CompilerParams(vmem_limit_bytes=VMEM_LIMIT),
        name="middle",
    )(received)


def run_last(received, factor):
    def kernel(*refs):
        last_kernel(factor, *refs)

    return pl.pallas_call(
        kernel,
        grid=(1,),
        out_shape=(jax.ShapeDtypeStruct((32, 72), F32), jax.ShapeDtypeStruct((24, 32), F32)),
        in_specs=[whole(8, 24, 128)],
        out_specs=(whole(32, 72), whole(24, 32)),
        compiler_params=pltpu.CompilerParams(vmem_limit_bytes=VMEM_LIMIT),
        name="last",
    )(received)


def local(video, saved, grad_out, spatial_w, temporal_w):
    shape = grad_out.shape
    grad = grad_out.reshape(4, PIX, C)
    saved = saved.reshape(4, PIX, C)
    video = video.reshape(4, PIX, C)
    back = [(i, i - 1) for i in range(1, 32)]
    halo_a = lax.ppermute(grad[0:1], "frame", back)
    halo_b = lax.ppermute(grad[1:2], "frame", back)
    gv, acc = run_first(grad, saved, video, spatial_w, temporal_w)
    gv, acc = run_third(grad, halo_a, saved, video, spatial_w, temporal_w, acc, gv)
    core = (lax.axis_index("frame") % 2).reshape(1)
    gv, send, keep = run_fourth(core, grad, halo_a, halo_b, saved, video, spatial_w, temporal_w, acc, gv)
    other = lax.ppermute(send, "frame", [(i, i ^ 1) for i in range(32)])
    chip = (keep.astype(F32) + other.astype(F32)).astype(BF16)
    planes = [[(d * 2 + y) * 16 + f for d in range(8) for y in range(2)] for f in range(16)]
    rows = lax.all_to_all(chip, ("dp", "frame"), 0, 0, tiled=True, axis_index_groups=planes)
    blocks = run_middle(rows)
    columns = [[y * 16 + z * 2 + c for z in range(8)] for y in range(2) for c in range(2)]
    owned = lax.all_to_all(blocks, "frame", 0, 0, tiled=True, axis_index_groups=columns)
    factor = 1.0 / math.sqrt(float(8 * 128 * 8 * 64))
    grad_spatial, grad_temporal = run_last(owned, factor)
    return (gv.reshape(shape), grad_spatial.T, grad_temporal)


def solution(mesh):
    return jax.shard_map(
        local,
        mesh=mesh,
        in_specs=(
            P("dp", "frame", None, None, None),
            P("dp", "frame", None, None, None),
            P("dp", "frame", None, None, None),
            P(),
            P(),
        ),
        out_specs=(P("dp", "frame", None, None, None), P("frame", "dp"), P("frame", "dp")),
        check_vma=False,
    )
```

```python
import math

import jax
import jax.numpy as jnp
from jax import lax
from jax.experimental import pallas as pl
from jax.experimental.pallas import tpu as pltpu
from jax.sharding import PartitionSpec as P


C = 256
WID = 64
PIX = 512
WS = 9 * C
WT = 3 * C
F32 = jnp.float32
BF16 = jnp.bfloat16
VMEM_LIMIT = 28 * 1024 * 1024


def dot_t(a, b):
    return lax.dot_general(a, b, (((1,), (1,)), ((), ())), preferred_element_type=F32)


def dot_n(a, b):
    return lax.dot_general(a, b, (((1,), (0,)), ((), ())), preferred_element_type=F32)


def fill_shifted(hidden, shifted_ref, frame):
    column = lax.broadcasted_iota(jnp.int32, (PIX, C), 0) % WID
    zeros = jnp.zeros((WID, C), BF16)
    right = jnp.where(column == 0, 0.0, pltpu.roll(hidden, 1, 0))
    left = jnp.where(column == WID - 1, 0.0, pltpu.roll(hidden, PIX - 1, 0))
    for slot, value in ((0, left), (1, hidden), (2, right)):
        shifted_ref[slot, frame, 0:WID] = zeros
        shifted_ref[slot, frame, WID : WID + PIX] = value.astype(BF16)
        shifted_ref[slot, frame, WID + PIX : 2 * WID + PIX] = zeros


def tap_rows(tap):
    row_off = tap // 3 - 1
    slot = tap % 3
    return slot, WID - WID * row_off


def video_gradient(shifted_ref, ws_w_ref, gv_ref):
    for frame in range(2):
        total = jnp.zeros((PIX, C), F32)
        for tap in range(9):
            slot, low = tap_rows(tap)
            total = total + dot_t(shifted_ref[slot, frame, low : low + PIX], ws_w_ref[tap * C : (tap + 1) * C])
        gv_ref[frame] = total.astype(BF16)


def tap_products(shifted_ref, video_ref, video_t_ref, emit):
    for frame in range(2):
        video_t_ref[:, frame * PIX : (frame + 1) * PIX] = video_ref[frame].T
    for tap in range(9):
        slot, low = tap_rows(tap)
        rows = shifted_ref[slot, :, low : low + PIX].reshape(2 * PIX, C)
        emit(tap, dot_n(video_t_ref[...], rows))


def hidden_of(frames, wt_w_ref):
    hidden = jnp.zeros((PIX, C), F32)
    for lag in range(3):
        hidden = hidden + dot_t(frames[lag], wt_w_ref[lag * C : (lag + 1) * C])
    return hidden


def first_kernel(
    grad_hbm, saved_hbm, video_hbm, ws_w_hbm, wt_w_hbm, gv_ref, acc_ref,
    grad_ref, saved_ref, video_ref, ws_w_ref, wt_w_ref, shifted_ref, video_t_ref, saved_t_ref, sems,
):
    sources = (saved_hbm, grad_hbm, wt_w_hbm, video_hbm.at[0:2], ws_w_hbm)
    targets = (saved_ref, grad_ref, wt_w_ref, video_ref, ws_w_ref)
    copies = [pltpu.make_async_copy(a, b, sems.at[i]) for i, (a, b) in enumerate(zip(sources, targets))]
    for copy in copies:
        copy.start()
    copies[0].wait()
    for frame in range(4):
        saved_t_ref[:, frame * PIX : (frame + 1) * PIX] = saved_ref[frame].T
    copies[1].wait()
    for lag in range(3):
        rows = grad_ref[lag:4].reshape((4 - lag) * PIX, C)
        acc_ref[WS + lag * C : WS + (lag + 1) * C] = dot_n(saved_t_ref[:, : (4 - lag) * PIX], rows)
    copies[2].wait()
    for frame in range(2):
        fill_shifted(hidden_of([grad_ref[frame + lag] for lag in range(3)], wt_w_ref), shifted_ref, frame)
    copies[3].wait()

    def emit(tap, value):
        acc_ref[tap * C : (tap + 1) * C] = value

    tap_products(shifted_ref, video_ref, video_t_ref, emit)
    copies[4].wait()
    video_gradient(shifted_ref, ws_w_ref, gv_ref)


def exchange(a, b, keep_a, rolls):
    crossed = jnp.where(keep_a, b, a)
    return (
        jnp.where(keep_a, a, pltpu.roll(crossed, rolls[0], 1)),
        jnp.where(keep_a, pltpu.roll(crossed, rolls[1], 1), b),
    )


def pack(total_ref, first_row, count, core, out_ref, out_row):
    group = lax.broadcasted_iota(jnp.int32, (count, 128), 1) // 32
    low_half, even = group < 2, group % 2 == 0
    for y_lo in range(2):
        for z_low in range(2):
            for half in range(2):
                parts = []
                for j in range(4):
                    row = pl.multiple_of(first_row + (((y_lo * 8 + 2 * j + z_low) * 2) + core) * count, 8)
                    parts.append(total_ref[pl.ds(row, count), half * 128 : (half + 1) * 128])
                low_0, high_0 = exchange(parts[0], parts[2], low_half, (64, 64))
                low_1, high_1 = exchange(parts[1], parts[3], low_half, (64, 64))
                values = exchange(low_0, low_1, even, (32, 96)) + exchange(high_0, high_1, even, (32, 96))
                low = out_row + z_low * count
                for dq in range(4):
                    out_ref[(half * 4 + dq) * 2 + y_lo, low : low + count] = values[dq].astype(BF16)


def second_kernel(
    core_ref, grad_ref, halo_ref, saved_ref, video_ref, wt_w_ref, acc_ref,
    send_ref, keep_ref, shifted_ref, video_t_ref, saved_t_ref, total_ref,
):
    frames = [grad_ref[0], grad_ref[1], halo_ref[0], halo_ref[1]]
    for frame in range(2):
        fill_shifted(hidden_of(frames[frame : frame + 3], wt_w_ref), shifted_ref, frame)
        saved_t_ref[:, frame * PIX : (frame + 1) * PIX] = saved_ref[frame].T
    total_ref[WS : WS + C] = acc_ref[WS : WS + C]
    total_ref[WS + C : WS + 2 * C] = acc_ref[WS + C : WS + 2 * C] + dot_n(saved_t_ref[:, PIX:], halo_ref[0])
    total_ref[WS + 2 * C :] = acc_ref[WS + 2 * C :] + dot_n(saved_t_ref[...], halo_ref[...].reshape(2 * PIX, C))

    def emit(tap, value):
        total_ref[tap * C : (tap + 1) * C] = acc_ref[tap * C : (tap + 1) * C] + value

    tap_products(shifted_ref, video_ref, video_t_ref, emit)
    core = core_ref[0]
    for target, ref in ((1 - core, send_ref), (core, keep_ref)):
        pack(total_ref, 0, 72, target, ref, 0)
        pack(total_ref, WS, 24, target, ref, 144)


def values_kernel(shifted_ref, ws_w_ref, gv_in_ref, gv_ref):
    del gv_in_ref
    video_gradient(shifted_ref, ws_w_ref, gv_ref)


def middle_kernel(in_ref, out_ref, sum_ref):
    total = in_ref[0].astype(F32)
    for source in range(1, 16):
        total = total + in_ref[source].astype(F32)
    sum_ref[...] = total
    group = lax.broadcasted_iota(jnp.int32, (24, 128), 1) // 32
    for z_low in range(2):
        rows = [sum_ref[72 * z_low + 24 * g : 72 * z_low + 24 * (g + 1)] for g in range(3)]
        rows.append(sum_ref[144 + 24 * z_low : 144 + 24 * (z_low + 1)])
        for j in range(4):
            value = rows[j]
            for g in range(4):
                if g != j:
                    value = jnp.where(group == g, pltpu.roll(rows[g], ((g - j) * 32) % 128, 1), value)
            out_ref[2 * j + z_low] = value.astype(BF16)


def last_kernel(factor, in_ref, ws_ref, wt_ref):
    total = in_ref[0].astype(F32)
    for source in range(1, 8):
        total = total + in_ref[source].astype(F32)
    total = total * factor
    for g in range(3):
        ws_ref[:, 24 * g : 24 * (g + 1)] = total[:, 32 * g : 32 * (g + 1)].T
    wt_ref[...] = total[:, 96:128]


def frames_spec(index, count=2):
    return pl.BlockSpec((count, PIX, C), lambda i: (index, 0, 0))


def whole(*shape):
    return pl.BlockSpec(shape, lambda i: (0,) * len(shape))


def in_place():
    return pl.BlockSpec(memory_space=pltpu.MemorySpace.HBM)


def run_first(grad, saved, video, ws_w, wt_w):
    return pl.pallas_call(
        first_kernel,
        grid=(1,),
        out_shape=(jax.ShapeDtypeStruct((4, PIX, C), BF16), jax.ShapeDtypeStruct((WS + WT, C), F32)),
        in_specs=[in_place()] * 5,
        out_specs=(frames_spec(0), whole(WS + WT, C)),
        scratch_shapes=[
            pltpu.VMEM((4, PIX, C), BF16),
            pltpu.VMEM((4, PIX, C), BF16),
            pltpu.VMEM((2, PIX, C), BF16),
            pltpu.VMEM((WS, C), BF16),
            pltpu.VMEM((WT, C), BF16),
            pltpu.VMEM((3, 2, PIX + 2 * WID, C), BF16),
            pltpu.VMEM((C, 2 * PIX), BF16),
            pltpu.VMEM((C, 4 * PIX), BF16),
            pltpu.SemaphoreType.DMA((5,)),
        ],
        compiler_params=pltpu.CompilerParams(vmem_limit_bytes=VMEM_LIMIT),
        cost_estimate=pl.CostEstimate(flops=4_000_000_000, bytes_accessed=8_000_000, transcendentals=0),
        name="first",
    )(grad, saved, video, ws_w, wt_w)


def run_second(core, grad, halo, saved, video, wt_w, acc):
    packed = jax.ShapeDtypeStruct((16, 192, 128), BF16)
    shifted = (3, 2, PIX + 2 * WID, C)
    return pl.pallas_call(
        second_kernel,
        grid=(1,),
        out_shape=(packed, packed, jax.ShapeDtypeStruct(shifted, BF16)),
        in_specs=[
            pl.BlockSpec(memory_space=pltpu.MemorySpace.SMEM), frames_spec(1), frames_spec(0), frames_spec(1), frames_spec(1),
            whole(WT, C), whole(WS + WT, C),
        ],
        out_specs=(whole(16, 192, 128), whole(16, 192, 128), whole(*shifted)),
        scratch_shapes=[
            pltpu.VMEM((C, 2 * PIX), BF16),
            pltpu.VMEM((C, 2 * PIX), BF16),
            pltpu.VMEM((WS + WT, C), F32),
        ],
        compiler_params=pltpu.CompilerParams(vmem_limit_bytes=VMEM_LIMIT),
        cost_estimate=pl.CostEstimate(flops=2_000_000_000, bytes_accessed=5_000_000, transcendentals=0),
        name="second",
    )(core, grad, halo, saved, video, wt_w, acc)


def run_values(shifted, ws_w, gv):
    return pl.pallas_call(
        values_kernel,
        grid=(1,),
        out_shape=jax.ShapeDtypeStruct((4, PIX, C), BF16),
        in_specs=[whole(3, 2, PIX + 2 * WID, C), whole(WS, C), pl.BlockSpec(memory_space=pl.ANY)],
        out_specs=frames_spec(1),
        input_output_aliases={2: 0},
        compiler_params=pltpu.CompilerParams(vmem_limit_bytes=VMEM_LIMIT),
        cost_estimate=pl.CostEstimate(flops=1_300_000_000, bytes_accessed=3_000_000, transcendentals=0),
        name="values",
    )(shifted, ws_w, gv)


def run_middle(received):
    return pl.pallas_call(
        middle_kernel,
        grid=(1,),
        out_shape=jax.ShapeDtypeStruct((8, 24, 128), BF16),
        in_specs=[whole(16, 192, 128)],
        out_specs=whole(8, 24, 128),
        scratch_shapes=[pltpu.VMEM((192, 128), F32)],
        compiler_params=pltpu.CompilerParams(vmem_limit_bytes=VMEM_LIMIT),
        name="middle",
    )(received)


def run_last(received, factor):
    def kernel(*refs):
        last_kernel(factor, *refs)

    return pl.pallas_call(
        kernel,
        grid=(1,),
        out_shape=(jax.ShapeDtypeStruct((32, 72), F32), jax.ShapeDtypeStruct((24, 32), F32)),
        in_specs=[whole(8, 24, 128)],
        out_specs=(whole(32, 72), whole(24, 32)),
        compiler_params=pltpu.CompilerParams(vmem_limit_bytes=VMEM_LIMIT),
        name="last",
    )(received)


def local(video, saved, grad_out, spatial_w, temporal_w):
    shape = grad_out.shape
    grad = grad_out.reshape(4, PIX, C)
    saved = saved.reshape(4, PIX, C)
    video = video.reshape(4, PIX, C)
    halo = lax.ppermute(grad[0:2], "frame", [(i, i - 1) for i in range(1, 32)])
    held = [pltpu.with_memory_space_constraint(x, pltpu.MemorySpace.HBM) for x in (grad, saved, video, spatial_w, temporal_w)]
    gv, acc = run_first(*held)
    core = (lax.axis_index("frame") & 1).reshape(1)
    send, keep, shifted = run_second(core, grad, halo, saved, video, temporal_w, acc)
    gv = run_values(shifted, spatial_w, gv)
    other = lax.ppermute(send, "frame", [(i, i ^ 1) for i in range(32)])
    chip = (keep.astype(F32) + other.astype(F32)).astype(BF16)
    planes = [[(d * 2 + y) * 16 + f for d in range(8) for y in range(2)] for f in range(16)]
    rows = lax.all_to_all(chip, ("dp", "frame"), 0, 0, tiled=True, axis_index_groups=planes)
    blocks = run_middle(rows)
    columns = [[y * 16 + z * 2 + c for z in range(8)] for y in range(2) for c in range(2)]
    owned = lax.all_to_all(blocks, "frame", 0, 0, tiled=True, axis_index_groups=columns)
    factor = 1.0 / math.sqrt(float(8 * 128 * 8 * 64))
    grad_spatial, grad_temporal = run_last(owned, factor)
    return (gv.reshape(shape), grad_spatial.T, grad_temporal)


def solution(mesh):
    return jax.shard_map(
        local,
        mesh=mesh,
        in_specs=(
            P("dp", "frame", None, None, None),
            P("dp", "frame", None, None, None),
            P("dp", "frame", None, None, None),
            P(),
            P(),
        ),
        out_specs=(P("dp", "frame", None, None, None), P("frame", "dp"), P("frame", "dp")),
        check_vma=False,
    )
```

```python
import math

import jax
import jax.numpy as jnp
from jax import lax
from jax.experimental import pallas as pl
from jax.experimental.pallas import tpu as pltpu
from jax.sharding import PartitionSpec as P


C = 256
WID = 64
PIX = 512
WS = 9 * C
WT = 3 * C
F32 = jnp.float32
BF16 = jnp.bfloat16
VMEM_LIMIT = 28 * 1024 * 1024


def dot_t(a, b):
    return lax.dot_general(a, b, (((1,), (1,)), ((), ())), preferred_element_type=F32)


def dot_n(a, b):
    return lax.dot_general(a, b, (((1,), (0,)), ((), ())), preferred_element_type=F32)


def fill_shifted(hidden, shifted_ref, frame):
    column = lax.broadcasted_iota(jnp.int32, (PIX, C), 0) % WID
    zeros = jnp.zeros((WID, C), BF16)
    right = jnp.where(column == 0, 0.0, pltpu.roll(hidden, 1, 0))
    left = jnp.where(column == WID - 1, 0.0, pltpu.roll(hidden, PIX - 1, 0))
    for slot, value in ((0, left), (1, hidden), (2, right)):
        shifted_ref[slot, frame, 0:WID] = zeros
        shifted_ref[slot, frame, WID : WID + PIX] = value.astype(BF16)
        shifted_ref[slot, frame, WID + PIX : 2 * WID + PIX] = zeros


def tap_rows(tap):
    row_off = tap // 3 - 1
    slot = tap % 3
    return slot, WID - WID * row_off


def video_gradient(shifted_ref, ws_w_ref, gv_ref):
    for frame in range(2):
        total = jnp.zeros((PIX, C), F32)
        for tap in range(9):
            slot, low = tap_rows(tap)
            total = total + dot_t(shifted_ref[slot, frame, low : low + PIX], ws_w_ref[tap * C : (tap + 1) * C])
        gv_ref[frame] = total.astype(BF16)


def tap_products(shifted_ref, video_t, emit):
    for tap in range(9):
        slot, low = tap_rows(tap)
        rows = shifted_ref[slot, :, low : low + PIX].reshape(2 * PIX, C)
        emit(tap, dot_n(video_t, rows))


def hidden_of(frames, wt_w_ref):
    hidden = jnp.zeros((PIX, C), F32)
    for lag in range(3):
        hidden = hidden + dot_t(frames[lag], wt_w_ref[lag * C : (lag + 1) * C])
    return hidden


def first_kernel(
    grad_hbm, saved_hbm, video_hbm, ws_w_hbm, wt_w_hbm,
    gv_hbm, acc_ref, grad_ref, saved_t_ref, video_t_ref, ws_w_ref, wt_w_ref,
    saved_ref, video_ref, gv_ref, shifted_ref, sems,
):
    sources = (saved_hbm, grad_hbm, wt_w_hbm, video_hbm, ws_w_hbm)
    targets = (saved_ref, grad_ref, wt_w_ref, video_ref, ws_w_ref)
    copies = [pltpu.make_async_copy(a, b, sems.at[i]) for i, (a, b) in enumerate(zip(sources, targets))]
    for copy in copies:
        copy.start()
    copies[0].wait()
    for frame in range(4):
        saved_t_ref[:, frame * PIX : (frame + 1) * PIX] = saved_ref[frame].T
    copies[1].wait()
    for lag in range(3):
        rows = grad_ref[lag:4].reshape((4 - lag) * PIX, C)
        acc_ref[WS + lag * C : WS + (lag + 1) * C] = dot_n(saved_t_ref[:, : (4 - lag) * PIX], rows)
    copies[2].wait()
    for frame in range(2):
        fill_shifted(hidden_of([grad_ref[frame + lag] for lag in range(3)], wt_w_ref), shifted_ref, frame)
    copies[3].wait()
    for frame in range(4):
        video_t_ref[:, frame * PIX : (frame + 1) * PIX] = video_ref[frame].T
    copies[4].wait()
    video_gradient(shifted_ref, ws_w_ref, gv_ref)
    out = pltpu.make_async_copy(gv_ref, gv_hbm.at[0:2], sems.at[5])
    out.start()

    def emit(tap, value):
        acc_ref[tap * C : (tap + 1) * C] = value

    tap_products(shifted_ref, video_t_ref[:, : 2 * PIX], emit)
    out.wait()


def exchange(a, b, keep_a, rolls):
    crossed = jnp.where(keep_a, b, a)
    return (
        jnp.where(keep_a, a, pltpu.roll(crossed, rolls[0], 1)),
        jnp.where(keep_a, pltpu.roll(crossed, rolls[1], 1), b),
    )


def pack(total_ref, first_row, count, core, out_ref, out_row):
    group = lax.broadcasted_iota(jnp.int32, (count, 128), 1) // 32
    low_half, even = group < 2, group % 2 == 0
    for y_lo in range(2):
        for z_low in range(2):
            for half in range(2):
                parts = []
                for j in range(4):
                    row = pl.multiple_of(first_row + (((y_lo * 8 + 2 * j + z_low) * 2) + core) * count, 8)
                    parts.append(total_ref[pl.ds(row, count), half * 128 : (half + 1) * 128])
                low_0, high_0 = exchange(parts[0], parts[2], low_half, (64, 64))
                low_1, high_1 = exchange(parts[1], parts[3], low_half, (64, 64))
                values = exchange(low_0, low_1, even, (32, 96)) + exchange(high_0, high_1, even, (32, 96))
                low = out_row + z_low * count
                for dq in range(4):
                    out_ref[(half * 4 + dq) * 2 + y_lo, low : low + count] = values[dq].astype(BF16)


def second_kernel(
    core_ref, grad_ref, halo_ref, saved_t_ref, video_t_ref, wt_w_ref, acc_ref,
    send_ref, keep_ref, shifted_ref, total_ref,
):
    frames = [grad_ref[2], grad_ref[3], halo_ref[0], halo_ref[1]]
    for frame in range(2):
        fill_shifted(hidden_of(frames[frame : frame + 3], wt_w_ref), shifted_ref, frame)
    total_ref[WS : WS + C] = acc_ref[WS : WS + C]
    total_ref[WS + C : WS + 2 * C] = acc_ref[WS + C : WS + 2 * C] + dot_n(saved_t_ref[:, 3 * PIX :], halo_ref[0])
    total_ref[WS + 2 * C :] = acc_ref[WS + 2 * C :] + dot_n(saved_t_ref[:, 2 * PIX :], halo_ref[...].reshape(2 * PIX, C))

    def emit(tap, value):
        total_ref[tap * C : (tap + 1) * C] = acc_ref[tap * C : (tap + 1) * C] + value

    tap_products(shifted_ref, video_t_ref[:, 2 * PIX :], emit)
    core = core_ref[0]
    for target, ref in ((1 - core, send_ref), (core, keep_ref)):
        pack(total_ref, 0, 72, target, ref, 0)
        pack(total_ref, WS, 24, target, ref, 144)


def values_kernel(shifted_ref, ws_w_ref, gv_in_ref, gv_hbm, gv_ref, sem):
    del gv_in_ref
    video_gradient(shifted_ref, ws_w_ref, gv_ref)
    out = pltpu.make_async_copy(gv_ref, gv_hbm.at[2:4], sem)
    out.start()
    out.wait()


def middle_kernel(in_ref, out_ref, sum_ref):
    total = in_ref[0].astype(F32)
    for source in range(1, 16):
        total = total + in_ref[source].astype(F32)
    sum_ref[...] = total
    group = lax.broadcasted_iota(jnp.int32, (24, 128), 1) // 32
    for z_low in range(2):
        rows = [sum_ref[72 * z_low + 24 * g : 72 * z_low + 24 * (g + 1)] for g in range(3)]
        rows.append(sum_ref[144 + 24 * z_low : 144 + 24 * (z_low + 1)])
        for j in range(4):
            value = rows[j]
            for g in range(4):
                if g != j:
                    value = jnp.where(group == g, pltpu.roll(rows[g], ((g - j) * 32) % 128, 1), value)
            out_ref[2 * j + z_low] = value.astype(BF16)


def last_kernel(factor, in_ref, ws_ref, wt_ref):
    total = in_ref[0].astype(F32)
    for source in range(1, 8):
        total = total + in_ref[source].astype(F32)
    total = total * factor
    for g in range(3):
        ws_ref[:, 24 * g : 24 * (g + 1)] = total[:, 32 * g : 32 * (g + 1)].T
    wt_ref[...] = total[:, 96:128]


def call(kernel, name, inputs, outputs, scratch, flops=0, moved=0, aliases=None):
    spec = {"h": pltpu.MemorySpace.HBM, "v": pltpu.MemorySpace.VMEM, "s": pltpu.MemorySpace.SMEM}
    operands = [x if space == "s" else pltpu.with_memory_space_constraint(x, spec[space]) for x, space in inputs]
    return pl.pallas_call(
        kernel,
        out_shape=[jax.ShapeDtypeStruct(shape, kind) if space == "o" else spec[space](shape, kind) for shape, kind, space in outputs],
        in_specs=[pl.BlockSpec(memory_space=spec[space]) for _, space in inputs],
        out_specs=[pl.BlockSpec() if space == "o" else pl.BlockSpec(memory_space=spec[space]) for _, _, space in outputs],
        scratch_shapes=scratch,
        input_output_aliases=aliases or {},
        compiler_params=pltpu.CompilerParams(vmem_limit_bytes=VMEM_LIMIT),
        cost_estimate=pl.CostEstimate(flops=flops, bytes_accessed=moved, transcendentals=0),
        name=name,
    )(*operands)


SHIFTED = (3, 2, PIX + 2 * WID, C)
SLAB = (4, PIX, C)
HALF = (16, 192, 128)


def run_first(grad, saved, video, ws_w, wt_w):
    return call(
        first_kernel,
        "first",
        [(grad, "h"), (saved, "h"), (video, "h"), (ws_w, "h"), (wt_w, "h")],
        [
            (SLAB, BF16, "h"), ((WS + WT, C), F32, "v"), (SLAB, BF16, "v"), ((C, 4 * PIX), BF16, "v"), ((C, 4 * PIX), BF16, "v"),
            ((WS, C), BF16, "v"), ((WT, C), BF16, "v"),
        ],
        [
            pltpu.VMEM(SLAB, BF16),
            pltpu.VMEM(SLAB, BF16),
            pltpu.VMEM((2, PIX, C), BF16),
            pltpu.VMEM(SHIFTED, BF16),
            pltpu.SemaphoreType.DMA((6,)),
        ],
        flops=4_000_000_000,
        moved=5_000_000,
    )


def run_second(core, grad, halo, saved_t, video_t, wt_w, acc):
    return call(
        second_kernel,
        "second",
        [(core, "s"), (grad, "v"), (halo, "v"), (saved_t, "v"), (video_t, "v"), (wt_w, "v"), (acc, "v")],
        [(HALF, BF16, "v"), (HALF, BF16, "v"), (SHIFTED, BF16, "v")],
        [pltpu.VMEM((WS + WT, C), F32)],
        flops=2_000_000_000,
        moved=500_000,
    )


def run_values(shifted, ws_w, gv):
    return call(
        values_kernel,
        "values",
        [(shifted, "v"), (ws_w, "v"), (gv, "h")],
        [(SLAB, BF16, "h")],
        [pltpu.VMEM((2, PIX, C), BF16), pltpu.SemaphoreType.DMA],
        flops=1_300_000_000,
        moved=500_000,
        aliases={2: 0},
    )[0]


def run_middle(received):
    return call(
        middle_kernel, "middle", [(received, "v")], [((8, 24, 128), BF16, "v")], [pltpu.VMEM((192, 128), F32)], moved=100_000
    )[0]


def run_last(received, factor):
    def kernel(*refs):
        last_kernel(factor, *refs)

    return call(kernel, "last", [(received, "v")], [((32, 72), F32, "o"), ((24, 32), F32, "o")], [], moved=100_000)


def local(video, saved, grad_out, spatial_w, temporal_w):
    shape = grad_out.shape
    grad = grad_out.reshape(4, PIX, C)
    saved = saved.reshape(4, PIX, C)
    video = video.reshape(4, PIX, C)
    halo = lax.ppermute(grad[0:2], "frame", [(i, i - 1) for i in range(1, 32)])
    gv, acc, grad, saved_t, video_t, ws_w, wt_w = run_first(grad, saved, video, spatial_w, temporal_w)
    core = (lax.axis_index("frame") & 1).reshape(1)
    send, keep, shifted = run_second(core, grad, halo, saved_t, video_t, wt_w, acc)
    other = lax.ppermute(send, "frame", [(i, i ^ 1) for i in range(32)])
    gv = run_values(shifted, ws_w, gv)
    chip = (keep.astype(F32) + other.astype(F32)).astype(BF16)
    chip, gv = lax.optimization_barrier((chip, gv))
    planes = [[(d * 2 + y) * 16 + f for d in range(8) for y in range(2)] for f in range(16)]
    rows = lax.all_to_all(chip, ("dp", "frame"), 0, 0, tiled=True, axis_index_groups=planes)
    blocks = run_middle(rows)
    columns = [[y * 16 + z * 2 + c for z in range(8)] for y in range(2) for c in range(2)]
    owned = lax.all_to_all(blocks, "frame", 0, 0, tiled=True, axis_index_groups=columns)
    factor = 1.0 / math.sqrt(float(8 * 128 * 8 * 64))
    grad_spatial, grad_temporal = run_last(owned, factor)
    return (gv.reshape(shape), grad_spatial.T, grad_temporal)


def solution(mesh):
    return jax.shard_map(
        local,
        mesh=mesh,
        in_specs=(
            P("dp", "frame", None, None, None),
            P("dp", "frame", None, None, None),
            P("dp", "frame", None, None, None),
            P(),
            P(),
        ),
        out_specs=(P("dp", "frame", None, None, None), P("frame", "dp"), P("frame", "dp")),
        check_vma=False,
    )
```

```python
import math

import jax
import jax.numpy as jnp
from jax import lax
from jax.experimental import pallas as pl
from jax.experimental.pallas import tpu as pltpu
from jax.sharding import PartitionSpec as P


C = 256
WID = 64
PIX = 512
WS = 9 * C
WT = 3 * C
F32 = jnp.float32
BF16 = jnp.bfloat16
VMEM_LIMIT = 16 * 1024 * 1024


def dot_t(a, b):
    return lax.dot_general(a, b, (((1,), (1,)), ((), ())), preferred_element_type=F32)


def dot_n(a, b):
    return lax.dot_general(a, b, (((1,), (0,)), ((), ())), preferred_element_type=F32)


def fill_shifted(hidden, shifted_ref, frame):
    column = lax.broadcasted_iota(jnp.int32, (PIX, C), 0) % WID
    zeros = jnp.zeros((WID, C), BF16)
    right = jnp.where(column == 0, 0.0, pltpu.roll(hidden, 1, 0))
    left = jnp.where(column == WID - 1, 0.0, pltpu.roll(hidden, PIX - 1, 0))
    for slot, value in ((0, left), (1, hidden), (2, right)):
        shifted_ref[slot, frame, 0:WID] = zeros
        shifted_ref[slot, frame, WID : WID + PIX] = value.astype(BF16)
        shifted_ref[slot, frame, WID + PIX : 2 * WID + PIX] = zeros


def tap_rows(tap):
    row_off = tap // 3 - 1
    slot = tap % 3
    return slot, WID - WID * row_off


def tap_products(shifted_ref, frames, video_t, emit):
    for tap in range(9):
        slot, low = tap_rows(tap)
        rows = shifted_ref[slot, :, low : low + PIX].reshape(frames * PIX, C)
        emit(tap, dot_n(video_t, rows))


def hidden_of(frames, wt_w_ref):
    hidden = jnp.zeros((PIX, C), F32)
    for lag in range(3):
        hidden = hidden + dot_t(frames[lag], wt_w_ref[lag * C : (lag + 1) * C])
    return hidden


def cut_kernel(grad_hbm, a_ref, b_ref, sems):
    copies = [pltpu.make_async_copy(grad_hbm.at[i : i + 1], ref, sems.at[i]) for i, ref in enumerate((a_ref, b_ref))]
    for copy in copies:
        copy.start()
    for copy in copies:
        copy.wait()


def first_kernel(
    grad_hbm, saved_hbm, video_hbm, wt_w_hbm,
    acc_ref, grad_ref, saved_t_ref, video_t_ref, wt_w_ref, hidden_hbm,
    saved_ref, video_ref, shifted_ref, sems,
):
    sources = (saved_hbm, grad_hbm, wt_w_hbm, video_hbm)
    targets = (saved_ref, grad_ref, wt_w_ref, video_ref)
    copies = [pltpu.make_async_copy(a, b, sems.at[i]) for i, (a, b) in enumerate(zip(sources, targets))]
    for copy in copies:
        copy.start()
    copies[0].wait()
    for frame in range(4):
        saved_t_ref[:, frame * PIX : (frame + 1) * PIX] = saved_ref[frame].T
    copies[1].wait()
    for lag in range(3):
        rows = grad_ref[lag:4].reshape((4 - lag) * PIX, C)
        acc_ref[WS + lag * C : WS + (lag + 1) * C] = dot_n(saved_t_ref[:, : (4 - lag) * PIX], rows)
    copies[2].wait()
    for frame in range(2):
        fill_shifted(hidden_of([grad_ref[frame + lag] for lag in range(3)], wt_w_ref), shifted_ref, frame)
    out = pltpu.make_async_copy(shifted_ref.at[1, :, WID : WID + PIX], hidden_hbm, sems.at[4])
    out.start()
    copies[3].wait()
    for frame in range(4):
        video_t_ref[:, frame * PIX : (frame + 1) * PIX] = video_ref[frame].T

    def emit(tap, value):
        acc_ref[tap * C : (tap + 1) * C] = value

    tap_products(shifted_ref, 2, video_t_ref[:, : 2 * PIX], emit)
    out.wait()


def third_frame_kernel(
    grad_ref, halo_ref, saved_t_ref, video_t_ref, wt_w_ref, acc_ref, out_ref, hidden_hbm, shifted_ref, sem
):
    fill_shifted(hidden_of([grad_ref[2], grad_ref[3], halo_ref[0]], wt_w_ref), shifted_ref, 0)
    out = pltpu.make_async_copy(shifted_ref.at[1, :, WID : WID + PIX], hidden_hbm, sem)
    out.start()
    out_ref[WS : WS + C] = acc_ref[WS : WS + C]
    for lag in (1, 2):
        rows = slice(WS + lag * C, WS + (lag + 1) * C)
        low = (4 - lag) * PIX
        out_ref[rows] = acc_ref[rows] + dot_n(saved_t_ref[:, low : low + PIX], halo_ref[0])

    def emit(tap, value):
        out_ref[tap * C : (tap + 1) * C] = acc_ref[tap * C : (tap + 1) * C] + value

    tap_products(shifted_ref, 1, video_t_ref[:, 2 * PIX : 3 * PIX], emit)
    out.wait()


def exchange(a, b, keep_a, rolls):
    crossed = jnp.where(keep_a, b, a)
    return (
        jnp.where(keep_a, a, pltpu.roll(crossed, rolls[0], 1)),
        jnp.where(keep_a, pltpu.roll(crossed, rolls[1], 1), b),
    )


def pack(total_ref, first_row, count, core, out_ref, out_row):
    group = lax.broadcasted_iota(jnp.int32, (count, 128), 1) // 32
    low_half, even = group < 2, group % 2 == 0
    for y_lo in range(2):
        for z_low in range(2):
            for half in range(2):
                parts = []
                for j in range(4):
                    row = pl.multiple_of(first_row + (((y_lo * 8 + 2 * j + z_low) * 2) + core) * count, 8)
                    parts.append(total_ref[pl.ds(row, count), half * 128 : (half + 1) * 128])
                low_0, high_0 = exchange(parts[0], parts[2], low_half, (64, 64))
                low_1, high_1 = exchange(parts[1], parts[3], low_half, (64, 64))
                values = exchange(low_0, low_1, even, (32, 96)) + exchange(high_0, high_1, even, (32, 96))
                low = out_row + z_low * count
                for dq in range(4):
                    out_ref[(half * 4 + dq) * 2 + y_lo, low : low + count] = values[dq].astype(BF16)


def fourth_frame_kernel(
    core_ref, grad_ref, halo_a_ref, halo_b_ref, saved_t_ref, video_t_ref, wt_w_ref, acc_ref,
    send_ref, keep_ref, hidden_hbm, total_ref, shifted_ref, sem,
):
    fill_shifted(hidden_of([grad_ref[3], halo_a_ref[0], halo_b_ref[0]], wt_w_ref), shifted_ref, 0)
    out = pltpu.make_async_copy(shifted_ref.at[1, :, WID : WID + PIX], hidden_hbm, sem)
    out.start()
    total_ref[WS : WS + 2 * C] = acc_ref[WS : WS + 2 * C]
    total_ref[WS + 2 * C :] = acc_ref[WS + 2 * C :] + dot_n(saved_t_ref[:, 3 * PIX :], halo_b_ref[0])

    def emit(tap, value):
        total_ref[tap * C : (tap + 1) * C] = acc_ref[tap * C : (tap + 1) * C] + value

    tap_products(shifted_ref, 1, video_t_ref[:, 3 * PIX :], emit)
    core = core_ref[0]
    for target, ref in ((1 - core, send_ref), (core, keep_ref)):
        pack(total_ref, 0, 72, target, ref, 0)
        pack(total_ref, WS, 24, target, ref, 144)
    out.wait()


def values_kernel(pair_hbm, third_hbm, fourth_hbm, ws_w_hbm, gv_hbm, hidden_ref, ws_w_ref, gv_ref, shifted_ref, sems):
    sources = (pair_hbm, third_hbm, fourth_hbm, ws_w_hbm)
    targets = (hidden_ref.at[0:2], hidden_ref.at[2:3], hidden_ref.at[3:4], ws_w_ref)
    copies = [pltpu.make_async_copy(a, b, sems.at[i]) for i, (a, b) in enumerate(zip(sources, targets))]
    for copy in copies:
        copy.start()
    for copy in copies:
        copy.wait()
    results = []
    for frame in range(4):
        fill_shifted(hidden_ref[frame].astype(F32), shifted_ref, frame)
        total = jnp.zeros((PIX, C), F32)
        for tap in range(9):
            slot, low = tap_rows(tap)
            total = total + dot_t(shifted_ref[slot, frame, low : low + PIX], ws_w_ref[tap * C : (tap + 1) * C])
        gv_ref[frame] = total.astype(BF16)
        results.append(pltpu.make_async_copy(gv_ref.at[frame], gv_hbm.at[frame], sems.at[4 + frame]))
        results[-1].start()
    for copy in results:
        copy.wait()


def chip_sum_kernel(keep_ref, other_ref, out_ref):
    out_ref[...] = (keep_ref[...].astype(F32) + other_ref[...].astype(F32)).astype(BF16)


def middle_kernel(in_ref, out_ref, sum_ref):
    total = in_ref[0].astype(F32)
    for source in range(1, 16):
        total = total + in_ref[source].astype(F32)
    sum_ref[...] = total
    group = lax.broadcasted_iota(jnp.int32, (24, 128), 1) // 32
    for z_low in range(2):
        rows = [sum_ref[72 * z_low + 24 * g : 72 * z_low + 24 * (g + 1)] for g in range(3)]
        rows.append(sum_ref[144 + 24 * z_low : 144 + 24 * (z_low + 1)])
        for j in range(4):
            value = rows[j]
            for g in range(4):
                if g != j:
                    value = jnp.where(group == g, pltpu.roll(rows[g], ((g - j) * 32) % 128, 1), value)
            out_ref[2 * j + z_low] = value.astype(BF16)


def last_kernel(factor, in_ref, ws_ref, wt_ref):
    total = in_ref[0].astype(F32)
    for source in range(1, 8):
        total = total + in_ref[source].astype(F32)
    total = total * factor
    for g in range(3):
        ws_ref[:, 24 * g : 24 * (g + 1)] = total[:, 32 * g : 32 * (g + 1)].T
    wt_ref[...] = total[:, 96:128]


def call(kernel, name, inputs, outputs, scratch, flops=0, moved=0, aliases=None):
    spec = {"h": pltpu.MemorySpace.HBM, "v": pltpu.MemorySpace.VMEM, "s": pltpu.MemorySpace.SMEM}
    operands = [x if space == "s" else pltpu.with_memory_space_constraint(x, spec[space]) for x, space in inputs]
    return pl.pallas_call(
        kernel,
        out_shape=[jax.ShapeDtypeStruct(shape, kind) if space == "o" else spec[space](shape, kind) for shape, kind, space in outputs],
        in_specs=[pl.BlockSpec(memory_space=spec[space]) for _, space in inputs],
        out_specs=[pl.BlockSpec() if space == "o" else pl.BlockSpec(memory_space=spec[space]) for _, _, space in outputs],
        scratch_shapes=scratch,
        input_output_aliases=aliases or {},
        compiler_params=pltpu.CompilerParams(vmem_limit_bytes=VMEM_LIMIT),
        cost_estimate=pl.CostEstimate(flops=flops, bytes_accessed=moved, transcendentals=0),
        name=name,
    )(*operands)


SLAB = (4, PIX, C)
HALF = (16, 192, 128)
ACC = (WS + WT, C)
FRAME = (1, PIX, C)


def shifted_shape(frames):
    return (3, frames, PIX + 2 * WID, C)


def run_cut(grad):
    return call(
        cut_kernel, "cut", [(grad, "h")], [(FRAME, BF16, "v"), (FRAME, BF16, "v")], [pltpu.SemaphoreType.DMA((2,))], moved=1_000_000
    )


def run_first(grad, saved, video, wt_w):
    return call(
        first_kernel,
        "first",
        [(grad, "h"), (saved, "h"), (video, "h"), (wt_w, "h")],
        [
            (ACC, F32, "v"), (SLAB, BF16, "v"), ((C, 4 * PIX), BF16, "v"), ((C, 4 * PIX), BF16, "v"), ((WT, C), BF16, "v"),
            ((2, PIX, C), BF16, "h"),
        ],
        [pltpu.VMEM(SLAB, BF16), pltpu.VMEM(SLAB, BF16), pltpu.VMEM(shifted_shape(2), BF16), pltpu.SemaphoreType.DMA((5,))],
        flops=2_500_000_000,
        moved=4_000_000,
    )


def run_third(grad, halo, saved_t, video_t, wt_w, acc):
    return call(
        third_frame_kernel,
        "third_frame",
        [(x, "v") for x in (grad, halo, saved_t, video_t, wt_w, acc)],
        [(ACC, F32, "v"), (FRAME, BF16, "h")],
        [pltpu.VMEM(shifted_shape(1), BF16), pltpu.SemaphoreType.DMA],
        flops=1_000_000_000,
        moved=500_000,
    )


def run_fourth(core, grad, halo_a, halo_b, saved_t, video_t, wt_w, acc):
    return call(
        fourth_frame_kernel,
        "fourth_frame",
        [(core, "s")] + [(x, "v") for x in (grad, halo_a, halo_b, saved_t, video_t, wt_w, acc)],
        [(HALF, BF16, "v"), (HALF, BF16, "v"), (FRAME, BF16, "h")],
        [pltpu.VMEM(ACC, F32), pltpu.VMEM(shifted_shape(1), BF16), pltpu.SemaphoreType.DMA],
        flops=1_000_000_000,
        moved=500_000,
    )


def run_values(pair, third, fourth, ws_w):
    return call(
        values_kernel,
        "values",
        [(x, "h") for x in (pair, third, fourth, ws_w)],
        [(SLAB, BF16, "h")],
        [
            pltpu.VMEM(SLAB, BF16), pltpu.VMEM((WS, C), BF16), pltpu.VMEM(SLAB, BF16), pltpu.VMEM(shifted_shape(4), BF16),
            pltpu.SemaphoreType.DMA((8,)),
        ],
        flops=2_500_000_000,
        moved=1_000_000,
    )[0]


def run_middle(received):
    return call(
        middle_kernel, "middle", [(received, "v")], [((8, 24, 128), BF16, "v")], [pltpu.VMEM((192, 128), F32)], moved=100_000
    )[0]


def run_last(received, factor):
    def kernel(*refs):
        last_kernel(factor, *refs)

    return call(kernel, "last", [(received, "v")], [((32, 72), F32, "o"), ((24, 32), F32, "o")], [], moved=100_000)


def local(video, saved, grad_out, spatial_w, temporal_w):
    shape = grad_out.shape
    grad = grad_out.reshape(4, PIX, C)
    saved = saved.reshape(4, PIX, C)
    video = video.reshape(4, PIX, C)
    back = [(i, i - 1) for i in range(1, 32)]
    cut_a, cut_b = run_cut(grad)
    halo_a = lax.ppermute(cut_a, "frame", back)
    halo_b = lax.ppermute(cut_b, "frame", back)
    acc, grad, saved_t, video_t, wt_w, pair = run_first(grad, saved, video, temporal_w)
    acc, third = run_third(grad, halo_a, saved_t, video_t, wt_w, acc)
    core = (lax.axis_index("frame") & 1).reshape(1)
    send, keep, fourth = run_fourth(core, grad, halo_a, halo_b, saved_t, video_t, wt_w, acc)
    other = lax.ppermute(send, "frame", [(i, i ^ 1) for i in range(32)])
    gv = run_values(pair, third, fourth, spatial_w)
    chip = call(chip_sum_kernel, "chip_sum", [(keep, "v"), (other, "v")], [(HALF, BF16, "v")], [], moved=100_000)[0]
    planes = [[(d * 2 + y) * 16 + f for d in range(8) for y in range(2)] for f in range(16)]
    rows = lax.all_to_all(chip, ("dp", "frame"), 0, 0, tiled=True, axis_index_groups=planes)
    blocks = run_middle(rows)
    blocks, gv = lax.optimization_barrier((blocks, gv))
    columns = [[y * 16 + z * 2 + c for z in range(8)] for y in range(2) for c in range(2)]
    owned = lax.all_to_all(blocks, "frame", 0, 0, tiled=True, axis_index_groups=columns)
    factor = 1.0 / math.sqrt(float(8 * 128 * 8 * 64))
    grad_spatial, grad_temporal = run_last(owned, factor)
    return (gv.reshape(shape), grad_spatial.T, grad_temporal)


def solution(mesh):
    return jax.shard_map(
        local,
        mesh=mesh,
        in_specs=(
            P("dp", "frame", None, None, None),
            P("dp", "frame", None, None, None),
            P("dp", "frame", None, None, None),
            P(),
            P(),
        ),
        out_specs=(P("dp", "frame", None, None, None), P("frame", "dp"), P("frame", "dp")),
        check_vma=False,
    )
```

```python
import math

import jax
import jax.numpy as jnp
from jax import lax
from jax.experimental import pallas as pl
from jax.experimental.pallas import tpu as pltpu
from jax.sharding import PartitionSpec as P


C = 256
WID = 64
PIX = 512
WS = 9 * C
WT = 3 * C
F32 = jnp.float32
BF16 = jnp.bfloat16
VMEM_LIMIT = 16 * 1024 * 1024


def dot_t(a, b):
    return lax.dot_general(a, b, (((1,), (1,)), ((), ())), preferred_element_type=F32)


def dot_n(a, b):
    return lax.dot_general(a, b, (((1,), (0,)), ((), ())), preferred_element_type=F32)


def fill_shifted(hidden, shifted_ref, frame):
    column = lax.broadcasted_iota(jnp.int32, (PIX, C), 0) % WID
    zeros = jnp.zeros((WID, C), BF16)
    right = jnp.where(column == 0, 0.0, pltpu.roll(hidden, 1, 0))
    left = jnp.where(column == WID - 1, 0.0, pltpu.roll(hidden, PIX - 1, 0))
    for slot, value in ((0, left), (1, hidden), (2, right)):
        shifted_ref[slot, frame, 0:WID] = zeros
        shifted_ref[slot, frame, WID : WID + PIX] = value.astype(BF16)
        shifted_ref[slot, frame, WID + PIX : 2 * WID + PIX] = zeros


def tap_rows(tap):
    row_off = tap // 3 - 1
    slot = tap % 3
    return slot, WID - WID * row_off


def tap_products(shifted_ref, frames, video_t, emit):
    for tap in range(9):
        slot, low = tap_rows(tap)
        rows = shifted_ref[slot, :, low : low + PIX].reshape(frames * PIX, C)
        emit(tap, dot_n(video_t, rows))


def hidden_of(frames, wt_w_ref):
    hidden = jnp.zeros((PIX, C), F32)
    for lag in range(3):
        hidden = hidden + dot_t(frames[lag], wt_w_ref[lag * C : (lag + 1) * C])
    return hidden


def cut_kernel(grad_hbm, a_ref, b_ref, sems):
    copies = [pltpu.make_async_copy(grad_hbm.at[i : i + 1], ref, sems.at[i]) for i, ref in enumerate((a_ref, b_ref))]
    for copy in copies:
        copy.start()
    for copy in copies:
        copy.wait()


def first_kernel(
    grad_hbm, saved_hbm, video_hbm, wt_w_hbm,
    acc_ref, grad_ref, saved_t_ref, video_t_ref, wt_w_ref, hidden_ref,
    saved_ref, video_ref, shifted_ref, sems,
):
    sources = (saved_hbm, grad_hbm, wt_w_hbm, video_hbm)
    targets = (saved_ref, grad_ref, wt_w_ref, video_ref)
    copies = [pltpu.make_async_copy(a, b, sems.at[i]) for i, (a, b) in enumerate(zip(sources, targets))]
    for copy in copies:
        copy.start()
    copies[0].wait()
    for frame in range(4):
        saved_t_ref[:, frame * PIX : (frame + 1) * PIX] = saved_ref[frame].T
    copies[1].wait()
    for lag in range(3):
        rows = grad_ref[lag:4].reshape((4 - lag) * PIX, C)
        acc_ref[WS + lag * C : WS + (lag + 1) * C] = dot_n(saved_t_ref[:, : (4 - lag) * PIX], rows)
    copies[2].wait()
    for frame in range(2):
        fill_shifted(hidden_of([grad_ref[frame + lag] for lag in range(3)], wt_w_ref), shifted_ref, frame)
    hidden_ref[...] = shifted_ref[1, :, WID : WID + PIX]
    copies[3].wait()
    for frame in range(4):
        video_t_ref[:, frame * PIX : (frame + 1) * PIX] = video_ref[frame].T

    def emit(tap, value):
        acc_ref[tap * C : (tap + 1) * C] = value

    tap_products(shifted_ref, 2, video_t_ref[:, : 2 * PIX], emit)


def exchange(a, b, keep_a, rolls):
    crossed = jnp.where(keep_a, b, a)
    return (
        jnp.where(keep_a, a, pltpu.roll(crossed, rolls[0], 1)),
        jnp.where(keep_a, pltpu.roll(crossed, rolls[1], 1), b),
    )


def pack(total_ref, first_row, count, core, out_ref, out_row):
    group = lax.broadcasted_iota(jnp.int32, (2 * count, 128), 1) // 32
    low_half, even = group < 2, group % 2 == 0
    for y_lo in range(2):
        for half in range(2):
            parts = []
            for j in range(4):
                rows = [
                    total_ref[
                        pl.ds(pl.multiple_of(first_row + ((y_lo * 8 + 2 * j + z_low) * 2 + core) * count, 8), count),
                        half * 128 : (half + 1) * 128,
                    ]
                    for z_low in range(2)
                ]
                parts.append(jnp.concatenate(rows, axis=0).astype(BF16))
            low_0, high_0 = exchange(parts[0], parts[2], low_half, (64, 64))
            low_1, high_1 = exchange(parts[1], parts[3], low_half, (64, 64))
            values = exchange(low_0, low_1, even, (32, 96)) + exchange(high_0, high_1, even, (32, 96))
            for dq in range(4):
                out_ref[(half * 4 + dq) * 2 + y_lo, out_row : out_row + 2 * count] = values[dq].astype(BF16)


def pack_all(total_ref, core, out_ref):
    pack(total_ref, 0, 72, core, out_ref, 0)
    pack(total_ref, WS, 24, core, out_ref, 144)


def second_kernel(
    core_ref, grad_ref, halo_a_ref, halo_b_ref, saved_t_ref, video_t_ref, wt_w_ref, acc_ref,
    send_ref, total_ref, hidden_ref, shifted_ref,
):
    frames = [grad_ref[2], grad_ref[3], halo_a_ref[0], halo_b_ref[0]]
    for frame in range(2):
        fill_shifted(hidden_of(frames[frame : frame + 3], wt_w_ref), shifted_ref, frame)
    hidden_ref[...] = shifted_ref[1, :, WID : WID + PIX]
    total_ref[WS : WS + C] = acc_ref[WS : WS + C]
    total_ref[WS + C : WS + 2 * C] = acc_ref[WS + C : WS + 2 * C] + dot_n(saved_t_ref[:, 3 * PIX :], halo_a_ref[0])
    halo = jnp.concatenate([halo_a_ref[0], halo_b_ref[0]], axis=0)
    total_ref[WS + 2 * C :] = acc_ref[WS + 2 * C :] + dot_n(saved_t_ref[:, 2 * PIX :], halo)

    def emit(tap, value):
        total_ref[tap * C : (tap + 1) * C] = acc_ref[tap * C : (tap + 1) * C] + value

    tap_products(shifted_ref, 2, video_t_ref[:, 2 * PIX :], emit)
    pack_all(total_ref, 1 - core_ref[0], send_ref)


def keep_kernel(core_ref, total_ref, early_ref, late_ref, keep_ref, hidden_hbm, sems):
    copies = [
        pltpu.make_async_copy(ref, hidden_hbm.at[2 * i : 2 * i + 2], sems.at[i]) for i, ref in enumerate((early_ref, late_ref))
    ]
    for copy in copies:
        copy.start()
    pack_all(total_ref, core_ref[0], keep_ref)
    for copy in copies:
        copy.wait()


def values_kernel(hidden_hbm, ws_w_hbm, gv_hbm, hidden_ref, ws_w_ref, gv_ref, shifted_ref, sems):
    sources = (hidden_hbm, ws_w_hbm)
    targets = (hidden_ref, ws_w_ref)
    copies = [pltpu.make_async_copy(a, b, sems.at[i]) for i, (a, b) in enumerate(zip(sources, targets))]
    for copy in copies:
        copy.start()
    for copy in copies:
        copy.wait()
    results = []
    for frame in range(4):
        fill_shifted(hidden_ref[frame].astype(F32), shifted_ref, frame)
        total = jnp.zeros((PIX, C), F32)
        for tap in range(9):
            slot, low = tap_rows(tap)
            total = total + dot_t(shifted_ref[slot, frame, low : low + PIX], ws_w_ref[tap * C : (tap + 1) * C])
        gv_ref[frame] = total.astype(BF16)
        results.append(pltpu.make_async_copy(gv_ref.at[frame], gv_hbm.at[frame], sems.at[4 + frame]))
        results[-1].start()
    for copy in results:
        copy.wait()


def middle_kernel(in_ref, out_ref, sum_ref):
    total = in_ref[0].astype(F32)
    for source in range(1, 16):
        total = total + in_ref[source].astype(F32)
    sum_ref[...] = total
    group = lax.broadcasted_iota(jnp.int32, (24, 128), 1) // 32
    for z_low in range(2):
        rows = [sum_ref[72 * z_low + 24 * g : 72 * z_low + 24 * (g + 1)] for g in range(3)]
        rows.append(sum_ref[144 + 24 * z_low : 144 + 24 * (z_low + 1)])
        for j in range(4):
            value = rows[j]
            for g in range(4):
                if g != j:
                    value = jnp.where(group == g, pltpu.roll(rows[g], ((g - j) * 32) % 128, 1), value)
            out_ref[2 * j + z_low] = value.astype(BF16)


def last_kernel(factor, in_ref, ws_ref, wt_ref):
    total = in_ref[0].astype(F32)
    for source in range(1, 8):
        total = total + in_ref[source].astype(F32)
    total = total * factor
    for g in range(3):
        ws_ref[:, 24 * g : 24 * (g + 1)] = total[:, 32 * g : 32 * (g + 1)].T
    wt_ref[...] = total[:, 96:128]


def call(kernel, name, inputs, outputs, scratch, flops=0, moved=0, aliases=None):
    spec = {"h": pltpu.MemorySpace.HBM, "v": pltpu.MemorySpace.VMEM, "s": pltpu.MemorySpace.SMEM}
    operands = [x if space == "s" else pltpu.with_memory_space_constraint(x, spec[space]) for x, space in inputs]
    return pl.pallas_call(
        kernel,
        out_shape=[jax.ShapeDtypeStruct(shape, kind) if space == "o" else spec[space](shape, kind) for shape, kind, space in outputs],
        in_specs=[pl.BlockSpec(memory_space=spec[space]) for _, space in inputs],
        out_specs=[pl.BlockSpec() if space == "o" else pl.BlockSpec(memory_space=spec[space]) for _, _, space in outputs],
        scratch_shapes=scratch,
        input_output_aliases=aliases or {},
        compiler_params=pltpu.CompilerParams(vmem_limit_bytes=VMEM_LIMIT),
        cost_estimate=pl.CostEstimate(flops=flops, bytes_accessed=moved, transcendentals=0),
        name=name,
    )(*operands)


SLAB = (4, PIX, C)
HALF = (16, 192, 128)
ACC = (WS + WT, C)
FRAME = (1, PIX, C)


def shifted_shape(frames):
    return (3, frames, PIX + 2 * WID, C)


def run_cut(grad):
    return call(
        cut_kernel, "cut", [(grad, "h")], [(FRAME, BF16, "v"), (FRAME, BF16, "v")], [pltpu.SemaphoreType.DMA((2,))], moved=1_000_000
    )


def run_first(grad, saved, video, wt_w):
    return call(
        first_kernel,
        "first",
        [(grad, "h"), (saved, "h"), (video, "h"), (wt_w, "h")],
        [
            (ACC, F32, "v"), (SLAB, BF16, "v"), ((C, 4 * PIX), BF16, "v"), ((C, 4 * PIX), BF16, "v"), ((WT, C), BF16, "v"),
            ((2, PIX, C), BF16, "v"),
        ],
        [pltpu.VMEM(SLAB, BF16), pltpu.VMEM(SLAB, BF16), pltpu.VMEM(shifted_shape(2), BF16), pltpu.SemaphoreType.DMA((4,))],
        flops=2_500_000_000,
        moved=4_000_000,
    )


def run_second(core, grad, halo_a, halo_b, saved_t, video_t, wt_w, acc):
    return call(
        second_kernel,
        "second",
        [(core, "s")] + [(x, "v") for x in (grad, halo_a, halo_b, saved_t, video_t, wt_w, acc)],
        [(HALF, BF16, "v"), (ACC, F32, "v"), ((2, PIX, C), BF16, "v")],
        [pltpu.VMEM(shifted_shape(2), BF16)],
        flops=2_000_000_000,
        moved=500_000,
    )


def run_keep(core, total, early, late):
    return call(
        keep_kernel,
        "keep",
        [(core, "s"), (total, "v"), (early, "v"), (late, "v")],
        [(HALF, BF16, "v"), (SLAB, BF16, "h")],
        [pltpu.SemaphoreType.DMA((2,))],
        flops=500_000_000,
        moved=1_000_000,
    )


def run_values(hidden, ws_w):
    return call(
        values_kernel,
        "values",
        [(x, "h") for x in (hidden, ws_w)],
        [(SLAB, BF16, "h")],
        [
            pltpu.VMEM(SLAB, BF16), pltpu.VMEM((WS, C), BF16), pltpu.VMEM(SLAB, BF16), pltpu.VMEM(shifted_shape(4), BF16),
            pltpu.SemaphoreType.DMA((8,)),
        ],
        flops=2_500_000_000,
        moved=1_000_000,
    )[0]


def run_middle(received):
    return call(
        middle_kernel, "middle", [(received, "v")], [((8, 24, 128), BF16, "v")], [pltpu.VMEM((192, 128), F32)], moved=100_000
    )[0]


def run_last(received, factor):
    def kernel(*refs):
        last_kernel(factor, *refs)

    return call(kernel, "last", [(received, "v")], [((32, 72), F32, "o"), ((24, 32), F32, "o")], [], moved=100_000)


def local(video, saved, grad_out, spatial_w, temporal_w):
    shape = grad_out.shape
    grad = grad_out.reshape(4, PIX, C)
    saved = saved.reshape(4, PIX, C)
    video = video.reshape(4, PIX, C)
    back = [(i, i - 1) for i in range(1, 32)]
    cut_a, cut_b = run_cut(grad)
    halo_a = lax.ppermute(cut_a, "frame", back)
    halo_b = lax.ppermute(cut_b, "frame", back)
    acc, grad, saved_t, video_t, wt_w, early = run_first(grad, saved, video, temporal_w)
    core = (lax.axis_index("frame") & 1).reshape(1)
    send, total, late = run_second(core, grad, halo_a, halo_b, saved_t, video_t, wt_w, acc)
    other = lax.ppermute(send, "frame", [(i, i ^ 1) for i in range(32)])
    keep, hidden = run_keep(core, total, early, late)
    gv = run_values(hidden, spatial_w)
    chip = (keep.astype(F32) + other.astype(F32)).astype(BF16)
    planes = [[(d * 2 + y) * 16 + f for d in range(8) for y in range(2)] for f in range(16)]
    rows = lax.all_to_all(chip, ("dp", "frame"), 0, 0, tiled=True, axis_index_groups=planes)
    blocks = run_middle(rows)
    blocks, gv = lax.optimization_barrier((blocks, gv))
    columns = [[y * 16 + z * 2 + c for z in range(8)] for y in range(2) for c in range(2)]
    owned = lax.all_to_all(blocks, "frame", 0, 0, tiled=True, axis_index_groups=columns)
    factor = 1.0 / math.sqrt(float(8 * 128 * 8 * 64))
    grad_spatial, grad_temporal = run_last(owned, factor)
    return (gv.reshape(shape), grad_spatial.T, grad_temporal)


def solution(mesh):
    return jax.shard_map(
        local,
        mesh=mesh,
        in_specs=(
            P("dp", "frame", None, None, None),
            P("dp", "frame", None, None, None),
            P("dp", "frame", None, None, None),
            P(),
            P(),
        ),
        out_specs=(P("dp", "frame", None, None, None), P("frame", "dp"), P("frame", "dp")),
        check_vma=False,
    )
```

```python
import math

import jax
import jax.numpy as jnp
from jax import lax
from jax.experimental import pallas as pl
from jax.experimental.pallas import tpu as pltpu
from jax.sharding import PartitionSpec as P


C = 256
WID = 64
PIX = 512
WS = 9 * C
WT = 3 * C
F32 = jnp.float32
BF16 = jnp.bfloat16
VMEM_LIMIT = 24 * 1024 * 1024


def dot_t(a, b):
    return lax.dot_general(a, b, (((1,), (1,)), ((), ())), preferred_element_type=F32)


def dot_n(a, b):
    return lax.dot_general(a, b, (((1,), (0,)), ((), ())), preferred_element_type=F32)


def fill_shifted(hidden, shifted_ref, frame):
    column = lax.broadcasted_iota(jnp.int32, (PIX, C), 0) % WID
    zeros = jnp.zeros((WID, C), BF16)
    right = jnp.where(column == 0, 0.0, pltpu.roll(hidden, 1, 0))
    left = jnp.where(column == WID - 1, 0.0, pltpu.roll(hidden, PIX - 1, 0))
    for slot, value in ((0, left), (1, hidden), (2, right)):
        shifted_ref[slot, frame, 0:WID] = zeros
        shifted_ref[slot, frame, WID : WID + PIX] = value.astype(BF16)
        shifted_ref[slot, frame, WID + PIX : 2 * WID + PIX] = zeros


def tap_rows(tap):
    row_off = tap // 3 - 1
    slot = tap % 3
    return slot, WID - WID * row_off


def tap_products(shifted_ref, frames, video_t, emit):
    for tap in range(9):
        slot, low = tap_rows(tap)
        rows = shifted_ref[slot, :, low : low + PIX].reshape(frames * PIX, C)
        emit(tap, dot_n(video_t, rows))


def hidden_of(frames, wt_w_ref):
    hidden = jnp.zeros((PIX, C), F32)
    for lag in range(3):
        hidden = hidden + dot_t(frames[lag], wt_w_ref[lag * C : (lag + 1) * C])
    return hidden


def frame_gradient(shifted_ref, frame, ws_w_ref, gv_ref):
    total = jnp.zeros((PIX, C), F32)
    for tap in range(9):
        slot, low = tap_rows(tap)
        total = total + dot_t(shifted_ref[slot, frame, low : low + PIX], ws_w_ref[tap * C : (tap + 1) * C])
    gv_ref[frame] = total.astype(BF16)


def first_kernel(
    grad_hbm, saved_hbm, video_hbm, ws_w_hbm, wt_w_hbm,
    gv_hbm, acc_ref, grad_ref, saved_t_ref, video_t_ref, ws_w_ref, wt_w_ref,
    saved_ref, video_ref, gv_ref, shifted_ref, sems,
):
    sources = (saved_hbm, grad_hbm, wt_w_hbm, video_hbm, ws_w_hbm)
    targets = (saved_ref, grad_ref, wt_w_ref, video_ref, ws_w_ref)
    copies = [pltpu.make_async_copy(a, b, sems.at[i]) for i, (a, b) in enumerate(zip(sources, targets))]
    for copy in copies:
        copy.start()
    copies[0].wait()
    for frame in range(4):
        saved_t_ref[:, frame * PIX : (frame + 1) * PIX] = saved_ref[frame].T
    copies[1].wait()
    for lag in range(3):
        rows = grad_ref[lag:4].reshape((4 - lag) * PIX, C)
        acc_ref[WS + lag * C : WS + (lag + 1) * C] = dot_n(saved_t_ref[:, : (4 - lag) * PIX], rows)
    copies[2].wait()
    for frame in range(2):
        fill_shifted(hidden_of([grad_ref[frame + lag] for lag in range(3)], wt_w_ref), shifted_ref, frame)
    copies[3].wait()
    for frame in range(4):
        video_t_ref[:, frame * PIX : (frame + 1) * PIX] = video_ref[frame].T
    copies[4].wait()
    for frame in range(2):
        frame_gradient(shifted_ref, frame, ws_w_ref, gv_ref)
    out = pltpu.make_async_copy(gv_ref, gv_hbm.at[0:2], sems.at[5])
    out.start()

    def emit(tap, value):
        acc_ref[tap * C : (tap + 1) * C] = value

    tap_products(shifted_ref, 2, video_t_ref[:, : 2 * PIX], emit)
    out.wait()


def exchange(a, b, keep_a, rolls):
    crossed = jnp.where(keep_a, b, a)
    return (
        jnp.where(keep_a, a, pltpu.roll(crossed, rolls[0], 1)),
        jnp.where(keep_a, pltpu.roll(crossed, rolls[1], 1), b),
    )


def pack(total_ref, first_row, count, core, out_ref, out_row):
    group = lax.broadcasted_iota(jnp.int32, (2 * count, 128), 1) // 32
    low_half, even = group < 2, group % 2 == 0
    for y_lo in range(2):
        for half in range(2):
            parts = []
            for j in range(4):
                rows = [
                    total_ref[
                        pl.ds(pl.multiple_of(first_row + ((y_lo * 8 + 2 * j + z_low) * 2 + core) * count, 8), count),
                        half * 128 : (half + 1) * 128,
                    ]
                    for z_low in range(2)
                ]
                parts.append(jnp.concatenate(rows, axis=0).astype(BF16))
            low_0, high_0 = exchange(parts[0], parts[2], low_half, (64, 64))
            low_1, high_1 = exchange(parts[1], parts[3], low_half, (64, 64))
            values = exchange(low_0, low_1, even, (32, 96)) + exchange(high_0, high_1, even, (32, 96))
            for dq in range(4):
                out_ref[(half * 4 + dq) * 2 + y_lo, out_row : out_row + 2 * count] = values[dq].astype(BF16)


def pack_all(total_ref, core, out_ref):
    pack(total_ref, 0, 72, core, out_ref, 0)
    pack(total_ref, WS, 24, core, out_ref, 144)


def second_kernel(
    core_ref, grad_ref, halo_ref, saved_t_ref, video_t_ref, wt_w_ref, acc_ref,
    send_ref, total_ref, shifted_ref,
):
    frames = [grad_ref[2], grad_ref[3], halo_ref[0], halo_ref[1]]
    for frame in range(2):
        fill_shifted(hidden_of(frames[frame : frame + 3], wt_w_ref), shifted_ref, frame)
    total_ref[WS : WS + C] = acc_ref[WS : WS + C]
    total_ref[WS + C : WS + 2 * C] = acc_ref[WS + C : WS + 2 * C] + dot_n(saved_t_ref[:, 3 * PIX :], halo_ref[0])
    total_ref[WS + 2 * C :] = acc_ref[WS + 2 * C :] + dot_n(saved_t_ref[:, 2 * PIX :], halo_ref[...].reshape(2 * PIX, C))

    def emit(tap, value):
        total_ref[tap * C : (tap + 1) * C] = acc_ref[tap * C : (tap + 1) * C] + value

    tap_products(shifted_ref, 2, video_t_ref[:, 2 * PIX :], emit)
    pack_all(total_ref, 1 - core_ref[0], send_ref)


def window_kernel(core_ref, total_ref, shifted_ref, ws_w_ref, gv_in_ref, keep_ref, gv_hbm, gv_ref, sems):
    del gv_in_ref
    copies = []
    for frame in range(2):
        frame_gradient(shifted_ref, frame, ws_w_ref, gv_ref)
        copies.append(pltpu.make_async_copy(gv_ref.at[frame], gv_hbm.at[2 + frame], sems.at[frame]))
        copies[-1].start()
    pack_all(total_ref, core_ref[0], keep_ref)
    for copy in copies:
        copy.wait()


def middle_kernel(in_ref, out_ref, sum_ref):
    total = in_ref[0].astype(F32)
    for source in range(1, 16):
        total = total + in_ref[source].astype(F32)
    sum_ref[...] = total
    group = lax.broadcasted_iota(jnp.int32, (24, 128), 1) // 32
    for z_low in range(2):
        rows = [sum_ref[72 * z_low + 24 * g : 72 * z_low + 24 * (g + 1)] for g in range(3)]
        rows.append(sum_ref[144 + 24 * z_low : 144 + 24 * (z_low + 1)])
        for j in range(4):
            value = rows[j]
            for g in range(4):
                if g != j:
                    value = jnp.where(group == g, pltpu.roll(rows[g], ((g - j) * 32) % 128, 1), value)
            out_ref[2 * j + z_low] = value.astype(BF16)


def last_kernel(factor, in_ref, ws_ref, wt_ref):
    total = in_ref[0].astype(F32)
    for source in range(1, 8):
        total = total + in_ref[source].astype(F32)
    total = total * factor
    for g in range(3):
        ws_ref[:, 24 * g : 24 * (g + 1)] = total[:, 32 * g : 32 * (g + 1)].T
    wt_ref[...] = total[:, 96:128]


def call(kernel, name, inputs, outputs, scratch, flops=0, moved=0, aliases=None):
    spec = {"h": pltpu.MemorySpace.HBM, "v": pltpu.MemorySpace.VMEM, "s": pltpu.MemorySpace.SMEM}
    operands = [x if space == "s" else pltpu.with_memory_space_constraint(x, spec[space]) for x, space in inputs]
    return pl.pallas_call(
        kernel,
        out_shape=[jax.ShapeDtypeStruct(shape, kind) if space == "o" else spec[space](shape, kind) for shape, kind, space in outputs],
        in_specs=[pl.BlockSpec(memory_space=spec[space]) for _, space in inputs],
        out_specs=[pl.BlockSpec() if space == "o" else pl.BlockSpec(memory_space=spec[space]) for _, _, space in outputs],
        scratch_shapes=scratch,
        input_output_aliases=aliases or {},
        compiler_params=pltpu.CompilerParams(vmem_limit_bytes=VMEM_LIMIT),
        cost_estimate=pl.CostEstimate(flops=flops, bytes_accessed=moved, transcendentals=0),
        name=name,
    )(*operands)


SLAB = (4, PIX, C)
HALF = (16, 192, 128)
ACC = (WS + WT, C)
SHIFTED = (3, 2, PIX + 2 * WID, C)


def run_first(grad, saved, video, ws_w, wt_w):
    return call(
        first_kernel,
        "first",
        [(grad, "h"), (saved, "h"), (video, "h"), (ws_w, "h"), (wt_w, "h")],
        [
            (SLAB, BF16, "h"), ((WS + WT, C), F32, "v"), (SLAB, BF16, "v"), ((C, 4 * PIX), BF16, "v"), ((C, 4 * PIX), BF16, "v"),
            ((WS, C), BF16, "v"), ((WT, C), BF16, "v"),
        ],
        [
            pltpu.VMEM(SLAB, BF16),
            pltpu.VMEM(SLAB, BF16),
            pltpu.VMEM((2, PIX, C), BF16),
            pltpu.VMEM(SHIFTED, BF16),
            pltpu.SemaphoreType.DMA((6,)),
        ],
        flops=4_000_000_000,
        moved=5_000_000,
    )


def run_second(core, grad, halo, saved_t, video_t, wt_w, acc):
    return call(
        second_kernel,
        "second",
        [(core, "s")] + [(x, "v") for x in (grad, halo, saved_t, video_t, wt_w, acc)],
        [(HALF, BF16, "v"), (ACC, F32, "v"), (SHIFTED, BF16, "v")],
        [],
        flops=2_000_000_000,
        moved=500_000,
    )


def run_window(core, total, shifted, ws_w, gv):
    return call(
        window_kernel,
        "window",
        [(core, "s"), (total, "v"), (shifted, "v"), (ws_w, "v"), (gv, "h")],
        [(HALF, BF16, "v"), (SLAB, BF16, "h")],
        [pltpu.VMEM((2, PIX, C), BF16), pltpu.SemaphoreType.DMA((2,))],
        flops=1_500_000_000,
        moved=1_000_000,
        aliases={4: 1},
    )


def run_middle(received):
    return call(
        middle_kernel, "middle", [(received, "v")], [((8, 24, 128), BF16, "v")], [pltpu.VMEM((192, 128), F32)], moved=100_000
    )[0]


def run_last(received, factor):
    def kernel(*refs):
        last_kernel(factor, *refs)

    return call(kernel, "last", [(received, "v")], [((32, 72), F32, "o"), ((24, 32), F32, "o")], [], moved=100_000)


def local(video, saved, grad_out, spatial_w, temporal_w):
    shape = grad_out.shape
    grad = grad_out.reshape(4, PIX, C)
    saved = saved.reshape(4, PIX, C)
    video = video.reshape(4, PIX, C)
    halo = lax.ppermute(grad[0:2], "frame", [(i, i - 1) for i in range(1, 32)])
    gv, acc, grad, saved_t, video_t, ws_w, wt_w = run_first(grad, saved, video, spatial_w, temporal_w)
    core = (lax.axis_index("frame") & 1).reshape(1)
    send, total, shifted = run_second(core, grad, halo, saved_t, video_t, wt_w, acc)
    other = lax.ppermute(send, "frame", [(i, i ^ 1) for i in range(32)])
    keep, gv = run_window(core, total, shifted, ws_w, gv)
    chip = (keep.astype(F32) + other.astype(F32)).astype(BF16)
    planes = [[(d * 2 + y) * 16 + f for d in range(8) for y in range(2)] for f in range(16)]
    rows = lax.all_to_all(chip, ("dp", "frame"), 0, 0, tiled=True, axis_index_groups=planes)
    blocks = run_middle(rows)
    columns = [[y * 16 + z * 2 + c for z in range(8)] for y in range(2) for c in range(2)]
    owned = lax.all_to_all(blocks, "frame", 0, 0, tiled=True, axis_index_groups=columns)
    factor = 1.0 / math.sqrt(float(8 * 128 * 8 * 64))
    grad_spatial, grad_temporal = run_last(owned, factor)
    return (gv.reshape(shape), grad_spatial.T, grad_temporal)


def solution(mesh):
    return jax.shard_map(
        local,
        mesh=mesh,
        in_specs=(
            P("dp", "frame", None, None, None),
            P("dp", "frame", None, None, None),
            P("dp", "frame", None, None, None),
            P(),
            P(),
        ),
        out_specs=(P("dp", "frame", None, None, None), P("frame", "dp"), P("frame", "dp")),
        check_vma=False,
    )
```

```python
import math

import jax
import jax.numpy as jnp
from jax import lax
from jax.experimental import pallas as pl
from jax.experimental.pallas import tpu as pltpu
from jax.sharding import PartitionSpec as P


C = 256
WID = 64
PIX = 512
WS = 9 * C
WT = 3 * C
F32 = jnp.float32
BF16 = jnp.bfloat16
VMEM_LIMIT = 24 * 1024 * 1024


def dot_t(a, b):
    return lax.dot_general(a, b, (((1,), (1,)), ((), ())), preferred_element_type=F32)


def dot_n(a, b):
    return lax.dot_general(a, b, (((1,), (0,)), ((), ())), preferred_element_type=F32)


def fill_shifted(hidden, shifted_ref, frame):
    column = lax.broadcasted_iota(jnp.int32, (PIX, C), 0) % WID
    zeros = jnp.zeros((WID, C), BF16)
    right = jnp.where(column == 0, 0.0, pltpu.roll(hidden, 1, 0))
    left = jnp.where(column == WID - 1, 0.0, pltpu.roll(hidden, PIX - 1, 0))
    for slot, value in ((0, left), (1, hidden), (2, right)):
        shifted_ref[slot, frame, 0:WID] = zeros
        shifted_ref[slot, frame, WID : WID + PIX] = value.astype(BF16)
        shifted_ref[slot, frame, WID + PIX : 2 * WID + PIX] = zeros


def tap_rows(tap):
    row_off = tap // 3 - 1
    slot = tap % 3
    return slot, WID - WID * row_off


def tap_products(shifted_ref, frames, video_t, emit):
    for tap in range(9):
        slot, low = tap_rows(tap)
        rows = shifted_ref[slot, :, low : low + PIX].reshape(frames * PIX, C)
        emit(tap, dot_n(video_t, rows))


def hidden_of(frames, wt_w_ref):
    hidden = jnp.zeros((PIX, C), F32)
    for lag in range(3):
        hidden = hidden + dot_t(frames[lag], wt_w_ref[lag * C : (lag + 1) * C])
    return hidden


def frame_gradient(shifted_ref, frame, ws_w_ref, gv_ref):
    total = jnp.zeros((PIX, C), F32)
    for tap in range(9):
        slot, low = tap_rows(tap)
        total = total + dot_t(shifted_ref[slot, frame, low : low + PIX], ws_w_ref[tap * C : (tap + 1) * C])
    gv_ref[frame] = total.astype(BF16)


def first_kernel(
    grad_hbm, saved_hbm, video_hbm, ws_w_hbm, wt_w_hbm,
    gv_hbm, acc_ref, begun_ref, saved_t_ref, video_t_ref, ws_w_ref, wt_w_ref,
    grad_ref, saved_ref, video_ref, gv_ref, shifted_ref, sems,
):
    sources = (saved_hbm, grad_hbm, wt_w_hbm, video_hbm, ws_w_hbm)
    targets = (saved_ref, grad_ref, wt_w_ref, video_ref, ws_w_ref)
    copies = [pltpu.make_async_copy(a, b, sems.at[i]) for i, (a, b) in enumerate(zip(sources, targets))]
    for copy in copies:
        copy.start()
    copies[0].wait()
    for frame in range(4):
        saved_t_ref[:, frame * PIX : (frame + 1) * PIX] = saved_ref[frame].T
    copies[1].wait()
    for lag in range(3):
        rows = grad_ref[lag:4].reshape((4 - lag) * PIX, C)
        acc_ref[WS + lag * C : WS + (lag + 1) * C] = dot_n(saved_t_ref[:, : (4 - lag) * PIX], rows)
    copies[2].wait()
    for frame in range(2):
        fill_shifted(hidden_of([grad_ref[frame + lag] for lag in range(3)], wt_w_ref), shifted_ref, frame)
    copies[3].wait()
    for frame in range(4):
        video_t_ref[:, frame * PIX : (frame + 1) * PIX] = video_ref[frame].T
    copies[4].wait()
    for frame in range(2):
        frame_gradient(shifted_ref, frame, ws_w_ref, gv_ref)
    out = pltpu.make_async_copy(gv_ref, gv_hbm.at[0:2], sems.at[5])
    out.start()

    def emit(tap, value):
        acc_ref[tap * C : (tap + 1) * C] = value

    tap_products(shifted_ref, 2, video_t_ref[:, : 2 * PIX], emit)
    weight = [wt_w_ref[lag * C : (lag + 1) * C] for lag in range(2)]
    begun_ref[0] = dot_t(grad_ref[2], weight[0]) + dot_t(grad_ref[3], weight[1])
    begun_ref[1] = dot_t(grad_ref[3], weight[0])
    out.wait()


def exchange(a, b, keep_a, rolls):
    crossed = jnp.where(keep_a, b, a)
    return (
        jnp.where(keep_a, a, pltpu.roll(crossed, rolls[0], 1)),
        jnp.where(keep_a, pltpu.roll(crossed, rolls[1], 1), b),
    )


def pack(total_ref, y_lo, count, core, out_ref, out_row, halves=(0, 1)):
    group = lax.broadcasted_iota(jnp.int32, (2 * count, 128), 1) // 32
    low_half, even = group < 2, group % 2 == 0
    for half in halves:
        parts = []
        for j in range(4):
            rows = [
                total_ref[
                    pl.ds(pl.multiple_of(((2 * j + z_low) * 2 + core) * count, 8), count), half * 128 : (half + 1) * 128
                ]
                for z_low in range(2)
            ]
            parts.append(jnp.concatenate(rows, axis=0).astype(BF16))
        low_0, high_0 = exchange(parts[0], parts[2], low_half, (64, 64))
        low_1, high_1 = exchange(parts[1], parts[3], low_half, (64, 64))
        values = exchange(low_0, low_1, even, (32, 96)) + exchange(high_0, high_1, even, (32, 96))
        for dq in range(4):
            out_ref[(half * 4 + dq) * 2 + y_lo, out_row : out_row + 2 * count] = values[dq]


def second_kernel(
    core_ref, begun_ref, halo_ref, saved_t_ref, video_t_ref, wt_w_ref, acc_ref,
    send_ref, ws_lo_ref, ws_hi_ref, wt_lo_ref, wt_hi_ref, shifted_ref,
):
    other = 1 - core_ref[0]
    weight = [wt_w_ref[lag * C : (lag + 1) * C] for lag in range(3)]
    fill_shifted(begun_ref[0] + dot_t(halo_ref[0], weight[2]), shifted_ref, 0)
    fill_shifted(begun_ref[1] + dot_t(halo_ref[0], weight[1]) + dot_t(halo_ref[1], weight[2]), shifted_ref, 1)
    middle = acc_ref[WS + C : WS + 2 * C] + dot_n(saved_t_ref[:, 3 * PIX :], halo_ref[0])
    wt_lo_ref[:C] = acc_ref[WS : WS + C]
    wt_lo_ref[C:] = middle[: C // 2]
    wt_hi_ref[: C // 2] = middle[C // 2 :]
    wt_hi_ref[C // 2 :] = acc_ref[WS + 2 * C :] + dot_n(saved_t_ref[:, 2 * PIX :], halo_ref[...].reshape(2 * PIX, C))
    video_t = video_t_ref[:, 2 * PIX :]

    def product(tap):
        slot, low = tap_rows(tap)
        rows = shifted_ref[slot, :, low : low + PIX].reshape(2 * PIX, C)
        return acc_ref[tap * C : (tap + 1) * C] + dot_n(video_t, rows)

    for tap in range(4):
        ws_lo_ref[tap * C : (tap + 1) * C] = product(tap)
        pack((wt_lo_ref, wt_hi_ref)[tap // 2], tap // 2, 24, other, send_ref, 144, (tap % 2,))
    centre = product(4)
    ws_lo_ref[4 * C :] = centre[: C // 2]
    ws_hi_ref[: C // 2] = centre[C // 2 :]
    for tap in range(5, 9):
        low = tap * C - WS // 2
        ws_hi_ref[low : low + C] = product(tap)
        if tap < 7:
            pack(ws_lo_ref, 0, 72, other, send_ref, 0, (tap - 5,))
    pack(ws_hi_ref, 1, 72, other, send_ref, 0)


def window_kernel(
    core_ref, ws_lo_ref, ws_hi_ref, wt_lo_ref, wt_hi_ref, shifted_ref, ws_w_ref, gv_in_ref, keep_ref, gv_hbm, gv_ref, sems
):
    del gv_in_ref
    copies = []
    for frame in range(2):
        frame_gradient(shifted_ref, frame, ws_w_ref, gv_ref)
        copies.append(pltpu.make_async_copy(gv_ref.at[frame], gv_hbm.at[2 + frame], sems.at[frame]))
        copies[-1].start()
    for y_lo, (ws_ref, wt_ref) in enumerate(((ws_lo_ref, wt_lo_ref), (ws_hi_ref, wt_hi_ref))):
        pack(ws_ref, y_lo, 72, core_ref[0], keep_ref, 0)
        pack(wt_ref, y_lo, 24, core_ref[0], keep_ref, 144)
    for copy in copies:
        copy.wait()


def middle_kernel(in_ref, out_ref, sum_ref):
    total = in_ref[0].astype(F32)
    for source in range(1, 16):
        total = total + in_ref[source].astype(F32)
    sum_ref[...] = total
    group = lax.broadcasted_iota(jnp.int32, (24, 128), 1) // 32
    for z_low in range(2):
        rows = [sum_ref[72 * z_low + 24 * g : 72 * z_low + 24 * (g + 1)] for g in range(3)]
        rows.append(sum_ref[144 + 24 * z_low : 144 + 24 * (z_low + 1)])
        for j in range(4):
            value = rows[j]
            for g in range(4):
                if g != j:
                    value = jnp.where(group == g, pltpu.roll(rows[g], ((g - j) * 32) % 128, 1), value)
            out_ref[2 * j + z_low] = value.astype(BF16)


def last_kernel(factor, in_ref, ws_ref, wt_ref):
    total = in_ref[0].astype(F32)
    for source in range(1, 8):
        total = total + in_ref[source].astype(F32)
    total = total * factor
    for g in range(3):
        ws_ref[:, 24 * g : 24 * (g + 1)] = total[:, 32 * g : 32 * (g + 1)].T
    wt_ref[...] = total[:, 96:128]


def call(kernel, name, inputs, outputs, scratch, flops=0, moved=0, aliases=None):
    spec = {"h": pltpu.MemorySpace.HBM, "v": pltpu.MemorySpace.VMEM, "s": pltpu.MemorySpace.SMEM}
    operands = [x if space == "s" else pltpu.with_memory_space_constraint(x, spec[space]) for x, space in inputs]
    return pl.pallas_call(
        kernel,
        out_shape=[jax.ShapeDtypeStruct(shape, kind) if space == "o" else spec[space](shape, kind) for shape, kind, space in outputs],
        in_specs=[pl.BlockSpec(memory_space=spec[space]) for _, space in inputs],
        out_specs=[pl.BlockSpec() if space == "o" else pl.BlockSpec(memory_space=spec[space]) for _, _, space in outputs],
        scratch_shapes=scratch,
        input_output_aliases=aliases or {},
        compiler_params=pltpu.CompilerParams(vmem_limit_bytes=VMEM_LIMIT),
        cost_estimate=pl.CostEstimate(flops=flops, bytes_accessed=moved, transcendentals=0),
        name=name,
    )(*operands)


SLAB = (4, PIX, C)
HALF = (16, 192, 128)
ACC = (WS + WT, C)
SHIFTED = (3, 2, PIX + 2 * WID, C)


def run_first(grad, saved, video, ws_w, wt_w):
    return call(
        first_kernel,
        "first",
        [(grad, "h"), (saved, "h"), (video, "h"), (ws_w, "h"), (wt_w, "h")],
        [
            (SLAB, BF16, "h"), ((WS + WT, C), F32, "v"), ((2, PIX, C), F32, "v"), ((C, 4 * PIX), BF16, "v"), ((C, 4 * PIX), BF16, "v"),
            ((WS, C), BF16, "v"), ((WT, C), BF16, "v"),
        ],
        [
            pltpu.VMEM(SLAB, BF16),
            pltpu.VMEM(SLAB, BF16),
            pltpu.VMEM(SLAB, BF16),
            pltpu.VMEM((2, PIX, C), BF16),
            pltpu.VMEM(SHIFTED, BF16),
            pltpu.SemaphoreType.DMA((6,)),
        ],
        flops=4_000_000_000,
        moved=5_000_000,
    )


def run_second(core, begun, halo, saved_t, video_t, wt_w, acc):
    return call(
        second_kernel,
        "second",
        [(core, "s")] + [(x, "v") for x in (begun, halo, saved_t, video_t, wt_w, acc)],
        [(HALF, BF16, "v")] + [((rows // 2, C), F32, "v") for rows in (WS, WS, WT, WT)] + [(SHIFTED, BF16, "v")],
        [],
        flops=2_000_000_000,
        moved=500_000,
    )


def run_window(core, totals, shifted, ws_w, gv):
    return call(
        window_kernel,
        "window",
        [(core, "s")] + [(x, "v") for x in totals] + [(shifted, "v"), (ws_w, "v"), (gv, "h")],
        [(HALF, BF16, "v"), (SLAB, BF16, "h")],
        [pltpu.VMEM((2, PIX, C), BF16), pltpu.SemaphoreType.DMA((2,))],
        flops=1_500_000_000,
        moved=1_000_000,
        aliases={7: 1},
    )


def run_middle(received):
    return call(
        middle_kernel, "middle", [(received, "v")], [((8, 24, 128), BF16, "v")], [pltpu.VMEM((192, 128), F32)], moved=100_000
    )[0]


def run_last(received, factor):
    def kernel(*refs):
        last_kernel(factor, *refs)

    return call(kernel, "last", [(received, "v")], [((32, 72), F32, "o"), ((24, 32), F32, "o")], [], moved=100_000)


def local(video, saved, grad_out, spatial_w, temporal_w):
    shape = grad_out.shape
    grad = grad_out.reshape(4, PIX, C)
    saved = saved.reshape(4, PIX, C)
    video = video.reshape(4, PIX, C)
    halo = lax.ppermute(grad[0:2], "frame", [(i, i - 1) for i in range(1, 32)])
    gv, acc, begun, saved_t, video_t, ws_w, wt_w = run_first(grad, saved, video, spatial_w, temporal_w)
    core = (lax.axis_index("frame") & 1).reshape(1)
    send, *totals, shifted = run_second(core, begun, halo, saved_t, video_t, wt_w, acc)
    other = lax.ppermute(send, "frame", [(i, i ^ 1) for i in range(32)])
    keep, gv = run_window(core, totals, shifted, ws_w, gv)
    chip = (keep.astype(F32) + other.astype(F32)).astype(BF16)
    planes = [[(d * 2 + y) * 16 + f for d in range(8) for y in range(2)] for f in range(16)]
    rows = lax.all_to_all(chip, ("dp", "frame"), 0, 0, tiled=True, axis_index_groups=planes)
    blocks = run_middle(rows)
    columns = [[y * 16 + z * 2 + c for z in range(8)] for y in range(2) for c in range(2)]
    owned = lax.all_to_all(blocks, "frame", 0, 0, tiled=True, axis_index_groups=columns)
    factor = 1.0 / math.sqrt(float(8 * 128 * 8 * 64))
    grad_spatial, grad_temporal = run_last(owned, factor)
    return (gv.reshape(shape), grad_spatial.T, grad_temporal)


def solution(mesh):
    return jax.shard_map(
        local,
        mesh=mesh,
        in_specs=(
            P("dp", "frame", None, None, None),
            P("dp", "frame", None, None, None),
            P("dp", "frame", None, None, None),
            P(),
            P(),
        ),
        out_specs=(P("dp", "frame", None, None, None), P("frame", "dp"), P("frame", "dp")),
        check_vma=False,
    )
```

```python
import math

import jax
import jax.numpy as jnp
from jax import lax
from jax.experimental import pallas as pl
from jax.experimental.pallas import tpu as pltpu
from jax.sharding import PartitionSpec as P


C = 256
WID = 64
PIX = 512
WS = 9 * C
WT = 3 * C
F32 = jnp.float32
BF16 = jnp.bfloat16
VMEM_LIMIT = 24 * 1024 * 1024


def dot_t(a, b):
    return lax.dot_general(a, b, (((1,), (1,)), ((), ())), preferred_element_type=F32)


def dot_n(a, b):
    return lax.dot_general(a, b, (((1,), (0,)), ((), ())), preferred_element_type=F32)


def fill_shifted(hidden, shifted_ref, frame):
    column = lax.broadcasted_iota(jnp.int32, (PIX, C), 0) % WID
    zeros = jnp.zeros((WID, C), BF16)
    right = jnp.where(column == 0, 0.0, pltpu.roll(hidden, 1, 0))
    left = jnp.where(column == WID - 1, 0.0, pltpu.roll(hidden, PIX - 1, 0))
    for slot, value in ((0, left), (1, hidden), (2, right)):
        shifted_ref[slot, frame, 0:WID] = zeros
        shifted_ref[slot, frame, WID : WID + PIX] = value.astype(BF16)
        shifted_ref[slot, frame, WID + PIX : 2 * WID + PIX] = zeros


def tap_rows(tap):
    row_off = tap // 3 - 1
    slot = tap % 3
    return slot, WID - WID * row_off


def tap_products(shifted_ref, frames, video_t, emit):
    for tap in range(9):
        slot, low = tap_rows(tap)
        rows = shifted_ref[slot, :, low : low + PIX].reshape(frames * PIX, C)
        emit(tap, dot_n(video_t, rows))


def hidden_of(frames, wt_w_ref):
    hidden = jnp.zeros((PIX, C), F32)
    for lag in range(3):
        hidden = hidden + dot_t(frames[lag], wt_w_ref[lag * C : (lag + 1) * C])
    return hidden


def frame_gradient(shifted_ref, frame, ws_w_ref, gv_ref):
    total = jnp.zeros((PIX, C), F32)
    for tap in range(9):
        slot, low = tap_rows(tap)
        total = total + dot_t(shifted_ref[slot, frame, low : low + PIX], ws_w_ref[tap * C : (tap + 1) * C])
    gv_ref[frame] = total.astype(BF16)


def first_kernel(
    grad_hbm, saved_hbm, video_hbm, ws_w_hbm, wt_w_hbm,
    gv_hbm, acc_ref, begun_ref, saved_t_ref, video_t_ref, ws_w_ref, wt_w_ref,
    grad_ref, saved_ref, video_ref, gv_ref, shifted_ref, sems,
):
    sources = (saved_hbm, grad_hbm, wt_w_hbm, video_hbm, ws_w_hbm)
    targets = (saved_ref, grad_ref, wt_w_ref, video_ref, ws_w_ref)
    copies = [pltpu.make_async_copy(a, b, sems.at[i]) for i, (a, b) in enumerate(zip(sources, targets))]
    for copy in copies:
        copy.start()
    copies[0].wait()
    for frame in range(4):
        saved_t_ref[:, frame * PIX : (frame + 1) * PIX] = saved_ref[frame].T
    copies[1].wait()
    for lag in range(3):
        rows = grad_ref[lag:4].reshape((4 - lag) * PIX, C)
        acc_ref[WS + lag * C : WS + (lag + 1) * C] = dot_n(saved_t_ref[:, : (4 - lag) * PIX], rows)
    copies[2].wait()
    for frame in range(2):
        fill_shifted(hidden_of([grad_ref[frame + lag] for lag in range(3)], wt_w_ref), shifted_ref, frame)
    copies[3].wait()
    for frame in range(4):
        video_t_ref[:, frame * PIX : (frame + 1) * PIX] = video_ref[frame].T
    copies[4].wait()
    for frame in range(2):
        frame_gradient(shifted_ref, frame, ws_w_ref, gv_ref)
    out = pltpu.make_async_copy(gv_ref, gv_hbm.at[0:2], sems.at[5])
    out.start()

    def emit(tap, value):
        acc_ref[tap * C : (tap + 1) * C] = value

    tap_products(shifted_ref, 2, video_t_ref[:, : 2 * PIX], emit)
    weight = [wt_w_ref[lag * C : (lag + 1) * C] for lag in range(2)]
    begun_ref[0] = dot_t(grad_ref[2], weight[0]) + dot_t(grad_ref[3], weight[1])
    begun_ref[1] = dot_t(grad_ref[3], weight[0])
    out.wait()


def exchange(a, b, keep_a, rolls):
    crossed = jnp.where(keep_a, b, a)
    return (
        jnp.where(keep_a, a, pltpu.roll(crossed, rolls[0], 1)),
        jnp.where(keep_a, pltpu.roll(crossed, rolls[1], 1), b),
    )


def slot_of(place_ref, core, x, y):
    ahead_x, ahead_y = (x - place_ref[1]) & 3, (y - place_ref[2]) & 3
    return jnp.where(core == 0, ahead_x * 4 + ahead_y, ahead_y * 4 + ahead_x)


def pack(total_ref, y_lo, count, place_ref, core, out_ref, out_row, halves=(0, 1)):
    group = lax.broadcasted_iota(jnp.int32, (2 * count, 128), 1) // 32
    low_half, even = group < 2, group % 2 == 0
    for half in halves:
        parts = []
        for j in range(4):
            rows = [
                total_ref[
                    pl.ds(pl.multiple_of(((2 * j + z_low) * 2 + core) * count, 8), count), half * 128 : (half + 1) * 128
                ]
                for z_low in range(2)
            ]
            parts.append(jnp.concatenate(rows, axis=0).astype(BF16))
        low_0, high_0 = exchange(parts[0], parts[2], low_half, (64, 64))
        low_1, high_1 = exchange(parts[1], parts[3], low_half, (64, 64))
        values = exchange(low_0, low_1, even, (32, 96)) + exchange(high_0, high_1, even, (32, 96))
        for dq in range(4):
            slot = slot_of(place_ref, core, dq, 2 * half + y_lo)
            out_ref[slot, out_row : out_row + 2 * count] = values[dq]


def second_kernel(
    place_ref, begun_ref, halo_ref, saved_t_ref, video_t_ref, wt_w_ref, acc_ref,
    send_ref, ws_lo_ref, ws_hi_ref, wt_lo_ref, wt_hi_ref, shifted_ref,
):
    other = 1 - place_ref[0]
    weight = [wt_w_ref[lag * C : (lag + 1) * C] for lag in range(3)]
    fill_shifted(begun_ref[0] + dot_t(halo_ref[0], weight[2]), shifted_ref, 0)
    fill_shifted(begun_ref[1] + dot_t(halo_ref[0], weight[1]) + dot_t(halo_ref[1], weight[2]), shifted_ref, 1)
    middle = acc_ref[WS + C : WS + 2 * C] + dot_n(saved_t_ref[:, 3 * PIX :], halo_ref[0])
    wt_lo_ref[:C] = acc_ref[WS : WS + C]
    wt_lo_ref[C:] = middle[: C // 2]
    wt_hi_ref[: C // 2] = middle[C // 2 :]
    wt_hi_ref[C // 2 :] = acc_ref[WS + 2 * C :] + dot_n(saved_t_ref[:, 2 * PIX :], halo_ref[...].reshape(2 * PIX, C))
    video_t = video_t_ref[:, 2 * PIX :]

    def product(tap):
        slot, low = tap_rows(tap)
        rows = shifted_ref[slot, :, low : low + PIX].reshape(2 * PIX, C)
        return acc_ref[tap * C : (tap + 1) * C] + dot_n(video_t, rows)

    for tap in range(4):
        ws_lo_ref[tap * C : (tap + 1) * C] = product(tap)
        pack((wt_lo_ref, wt_hi_ref)[tap // 2], tap // 2, 24, place_ref, other, send_ref, 144, (tap % 2,))
    centre = product(4)
    ws_lo_ref[4 * C :] = centre[: C // 2]
    ws_hi_ref[: C // 2] = centre[C // 2 :]
    for tap in range(5, 9):
        low = tap * C - WS // 2
        ws_hi_ref[low : low + C] = product(tap)
        if tap < 7:
            pack(ws_lo_ref, 0, 72, place_ref, other, send_ref, 0, (tap - 5,))
    pack(ws_hi_ref, 1, 72, place_ref, other, send_ref, 0)


def window_kernel(
    place_ref, ws_lo_ref, ws_hi_ref, wt_lo_ref, wt_hi_ref, shifted_ref, ws_w_ref, gv_in_ref, keep_ref, gv_hbm, gv_ref, sems
):
    del gv_in_ref
    copies = []
    for frame in range(2):
        frame_gradient(shifted_ref, frame, ws_w_ref, gv_ref)
        copies.append(pltpu.make_async_copy(gv_ref.at[frame], gv_hbm.at[2 + frame], sems.at[frame]))
        copies[-1].start()
    for y_lo, (ws_ref, wt_ref) in enumerate(((ws_lo_ref, wt_lo_ref), (ws_hi_ref, wt_hi_ref))):
        pack(ws_ref, y_lo, 72, place_ref, place_ref[0], keep_ref, 0)
        pack(wt_ref, y_lo, 24, place_ref, place_ref[0], keep_ref, 144)
    for copy in copies:
        copy.wait()


def chip_sum_kernel(keep_ref, other_ref, *out_refs):
    for step, out_ref in enumerate(out_refs):
        rows = slice(4 * step, 4 * step + 4)
        out_ref[...] = (keep_ref[rows].astype(F32) + other_ref[rows].astype(F32)).astype(BF16)


def line_sum_kernel(*refs):
    for step, out_ref in enumerate(refs[4:]):
        total = refs[0][step].astype(F32)
        for ref in refs[1:4]:
            total = total + ref[step].astype(F32)
        out_ref[...] = total.astype(BF16)


def middle_kernel(own_ref, *refs):
    out_ref, sum_ref = refs[3:]
    total = own_ref[...].astype(F32)
    for ref in refs[:3]:
        total = total + ref[...].astype(F32)
    sum_ref[...] = total
    group = lax.broadcasted_iota(jnp.int32, (24, 128), 1) // 32
    for z_low in range(2):
        rows = [sum_ref[72 * z_low + 24 * g : 72 * z_low + 24 * (g + 1)] for g in range(3)]
        rows.append(sum_ref[144 + 24 * z_low : 144 + 24 * (z_low + 1)])
        for j in range(4):
            value = rows[j]
            for g in range(4):
                if g != j:
                    value = jnp.where(group == g, pltpu.roll(rows[g], ((g - j) * 32) % 128, 1), value)
            out_ref[2 * j + z_low] = value.astype(BF16)


def last_kernel(factor, in_ref, ws_ref, wt_ref):
    total = in_ref[0].astype(F32)
    for source in range(1, 8):
        total = total + in_ref[source].astype(F32)
    total = total * factor
    for g in range(3):
        ws_ref[:, 24 * g : 24 * (g + 1)] = total[:, 32 * g : 32 * (g + 1)].T
    wt_ref[...] = total[:, 96:128]


def call(kernel, name, inputs, outputs, scratch, flops=0, moved=0, aliases=None):
    spec = {"h": pltpu.MemorySpace.HBM, "v": pltpu.MemorySpace.VMEM, "s": pltpu.MemorySpace.SMEM}
    operands = [x if space == "s" else pltpu.with_memory_space_constraint(x, spec[space]) for x, space in inputs]
    return pl.pallas_call(
        kernel,
        out_shape=[jax.ShapeDtypeStruct(shape, kind) if space == "o" else spec[space](shape, kind) for shape, kind, space in outputs],
        in_specs=[pl.BlockSpec(memory_space=spec[space]) for _, space in inputs],
        out_specs=[pl.BlockSpec() if space == "o" else pl.BlockSpec(memory_space=spec[space]) for _, _, space in outputs],
        scratch_shapes=scratch,
        input_output_aliases=aliases or {},
        compiler_params=pltpu.CompilerParams(vmem_limit_bytes=VMEM_LIMIT),
        cost_estimate=pl.CostEstimate(flops=flops, bytes_accessed=moved, transcendentals=0),
        name=name,
    )(*operands)


SLAB = (4, PIX, C)
HALF = (16, 192, 128)
ACC = (WS + WT, C)
SHIFTED = (3, 2, PIX + 2 * WID, C)


def run_first(grad, saved, video, ws_w, wt_w):
    return call(
        first_kernel,
        "first",
        [(grad, "h"), (saved, "h"), (video, "h"), (ws_w, "h"), (wt_w, "h")],
        [
            (SLAB, BF16, "h"), ((WS + WT, C), F32, "v"), ((2, PIX, C), F32, "v"), ((C, 4 * PIX), BF16, "v"), ((C, 4 * PIX), BF16, "v"),
            ((WS, C), BF16, "v"), ((WT, C), BF16, "v"),
        ],
        [
            pltpu.VMEM(SLAB, BF16),
            pltpu.VMEM(SLAB, BF16),
            pltpu.VMEM(SLAB, BF16),
            pltpu.VMEM((2, PIX, C), BF16),
            pltpu.VMEM(SHIFTED, BF16),
            pltpu.SemaphoreType.DMA((6,)),
        ],
        flops=4_000_000_000,
        moved=5_000_000,
    )


def run_second(place, begun, halo, saved_t, video_t, wt_w, acc):
    return call(
        second_kernel,
        "second",
        [(place, "s")] + [(x, "v") for x in (begun, halo, saved_t, video_t, wt_w, acc)],
        [(HALF, BF16, "v")] + [((rows // 2, C), F32, "v") for rows in (WS, WS, WT, WT)] + [(SHIFTED, BF16, "v")],
        [],
        flops=2_000_000_000,
        moved=500_000,
    )


def run_window(place, totals, shifted, ws_w, gv):
    return call(
        window_kernel,
        "window",
        [(place, "s")] + [(x, "v") for x in totals] + [(shifted, "v"), (ws_w, "v"), (gv, "h")],
        [(HALF, BF16, "v"), (SLAB, BF16, "h")],
        [pltpu.VMEM((2, PIX, C), BF16), pltpu.SemaphoreType.DMA((2,))],
        flops=1_500_000_000,
        moved=1_000_000,
        aliases={7: 1},
    )


def run_sum(kernel, name, arrays, shape):
    return call(kernel, name, [(x, "v") for x in arrays], [(shape, BF16, "v")] * 4, [], moved=100_000)


def run_middle(received):
    return call(
        middle_kernel, "middle", [(x, "v") for x in received], [((8, 24, 128), BF16, "v")], [pltpu.VMEM((192, 128), F32)], moved=100_000
    )[0]


def run_last(received, factor):
    def kernel(*refs):
        last_kernel(factor, *refs)

    return call(kernel, "last", [(received, "v")], [((32, 72), F32, "o"), ((24, 32), F32, "o")], [], moved=100_000)


def ahead(step, stage):
    pairs = []
    for device in range(256):
        group, member = divmod(device, 32)
        x, y, z, core = group % 4, (group // 4) * 2 + member // 16, (member // 2) % 8, member % 2
        if core == stage:
            x = (x + step) % 4
        else:
            y = (y + step) % 4
        pairs.append((device, ((y // 2) * 4 + x) * 32 + ((y % 2) * 8 + z) * 2 + core))
    return pairs


def local(video, saved, grad_out, spatial_w, temporal_w):
    shape = grad_out.shape
    grad = grad_out.reshape(4, PIX, C)
    saved = saved.reshape(4, PIX, C)
    video = video.reshape(4, PIX, C)
    halo = lax.ppermute(grad[0:2], "frame", [(i, i - 1) for i in range(1, 32)])
    gv, acc, begun, saved_t, video_t, ws_w, wt_w = run_first(grad, saved, video, spatial_w, temporal_w)
    group, member = lax.axis_index("dp"), lax.axis_index("frame")
    place = jnp.stack([member & 1, group & 3, (group >> 2) * 2 + (member >> 4)])
    send, *totals, shifted = run_second(place, begun, halo, saved_t, video_t, wt_w, acc)
    other = lax.ppermute(send, "frame", [(i, i ^ 1) for i in range(32)])
    keep, gv = run_window(place, totals, shifted, ws_w, gv)
    parts = run_sum(chip_sum_kernel, "chip_sum", (keep, other), (4, 192, 128))
    lines = [parts[0]] + [lax.ppermute(parts[k], ("dp", "frame"), ahead(k, 0)) for k in (1, 3, 2)]
    parts = run_sum(line_sum_kernel, "line_sum", lines, (192, 128))
    planes = [parts[0]] + [lax.ppermute(parts[k], ("dp", "frame"), ahead(k, 1)) for k in (1, 3, 2)]
    blocks = run_middle(planes)
    columns = [[y * 16 + z * 2 + c for z in range(8)] for y in range(2) for c in range(2)]
    owned = lax.all_to_all(blocks, "frame", 0, 0, tiled=True, axis_index_groups=columns)
    factor = 1.0 / math.sqrt(float(8 * 128 * 8 * 64))
    grad_spatial, grad_temporal = run_last(owned, factor)
    return (gv.reshape(shape), grad_spatial.T, grad_temporal)


def solution(mesh):
    return jax.shard_map(
        local,
        mesh=mesh,
        in_specs=(
            P("dp", "frame", None, None, None),
            P("dp", "frame", None, None, None),
            P("dp", "frame", None, None, None),
            P(),
            P(),
        ),
        out_specs=(P("dp", "frame", None, None, None), P("frame", "dp"), P("frame", "dp")),
        check_vma=False,
    )
```

```python
import math

import jax
import jax.numpy as jnp
from jax import lax
from jax.experimental import pallas as pl
from jax.experimental.pallas import tpu as pltpu
from jax.sharding import PartitionSpec as P


C = 256
WID = 64
PIX = 512
WS = 9 * C
WT = 3 * C
F32 = jnp.float32
BF16 = jnp.bfloat16
VMEM_LIMIT = 24 * 1024 * 1024


def dot_t(a, b):
    return lax.dot_general(a, b, (((1,), (1,)), ((), ())), preferred_element_type=F32)


def dot_n(a, b):
    return lax.dot_general(a, b, (((1,), (0,)), ((), ())), preferred_element_type=F32)


def fill_shifted(hidden, shifted_ref, frame):
    column = lax.broadcasted_iota(jnp.int32, (PIX, C), 0) % WID
    zeros = jnp.zeros((WID, C), BF16)
    right = jnp.where(column == 0, 0.0, pltpu.roll(hidden, 1, 0))
    left = jnp.where(column == WID - 1, 0.0, pltpu.roll(hidden, PIX - 1, 0))
    for slot, value in ((0, left), (1, hidden), (2, right)):
        shifted_ref[slot, frame, 0:WID] = zeros
        shifted_ref[slot, frame, WID : WID + PIX] = value.astype(BF16)
        shifted_ref[slot, frame, WID + PIX : 2 * WID + PIX] = zeros


def tap_rows(tap):
    row_off = tap // 3 - 1
    slot = tap % 3
    return slot, WID - WID * row_off


def tap_products(shifted_ref, frames, video_t, emit):
    for tap in range(9):
        slot, low = tap_rows(tap)
        rows = shifted_ref[slot, :, low : low + PIX].reshape(frames * PIX, C)
        emit(tap, dot_n(video_t, rows))


def hidden_of(frames, wt_w_ref):
    hidden = jnp.zeros((PIX, C), F32)
    for lag in range(3):
        hidden = hidden + dot_t(frames[lag], wt_w_ref[lag * C : (lag + 1) * C])
    return hidden


def frame_gradient(shifted_ref, frame, ws_w_ref, gv_ref):
    total = jnp.zeros((PIX, C), F32)
    for tap in range(9):
        slot, low = tap_rows(tap)
        total = total + dot_t(shifted_ref[slot, frame, low : low + PIX], ws_w_ref[tap * C : (tap + 1) * C])
    gv_ref[frame] = total.astype(BF16)


def first_kernel(
    grad_hbm, saved_hbm, video_hbm, ws_w_hbm, wt_w_hbm,
    gv_hbm, acc_ref, begun_ref, saved_t_ref, video_t_ref, ws_w_ref, wt_w_ref,
    grad_ref, saved_ref, video_ref, gv_ref, shifted_ref, sems,
):
    sources = (saved_hbm, grad_hbm, wt_w_hbm, video_hbm, ws_w_hbm)
    targets = (saved_ref, grad_ref, wt_w_ref, video_ref, ws_w_ref)
    copies = [pltpu.make_async_copy(a, b, sems.at[i]) for i, (a, b) in enumerate(zip(sources, targets))]
    for copy in copies:
        copy.start()
    copies[0].wait()
    for frame in range(4):
        saved_t_ref[:, frame * PIX : (frame + 1) * PIX] = saved_ref[frame].T
    copies[1].wait()
    for lag in range(3):
        rows = grad_ref[lag:4].reshape((4 - lag) * PIX, C)
        acc_ref[WS + lag * C : WS + (lag + 1) * C] = dot_n(saved_t_ref[:, : (4 - lag) * PIX], rows)
    copies[2].wait()
    for frame in range(2):
        fill_shifted(hidden_of([grad_ref[frame + lag] for lag in range(3)], wt_w_ref), shifted_ref, frame)
    copies[3].wait()
    for frame in range(4):
        video_t_ref[:, frame * PIX : (frame + 1) * PIX] = video_ref[frame].T
    copies[4].wait()
    for frame in range(2):
        frame_gradient(shifted_ref, frame, ws_w_ref, gv_ref)
    out = pltpu.make_async_copy(gv_ref, gv_hbm.at[0:2], sems.at[5])
    out.start()

    def emit(tap, value):
        acc_ref[tap * C : (tap + 1) * C] = value

    tap_products(shifted_ref, 2, video_t_ref[:, : 2 * PIX], emit)
    weight = [wt_w_ref[lag * C : (lag + 1) * C] for lag in range(2)]
    begun_ref[0] = dot_t(grad_ref[2], weight[0]) + dot_t(grad_ref[3], weight[1])
    begun_ref[1] = dot_t(grad_ref[3], weight[0])
    out.wait()


def exchange(a, b, keep_a, rolls):
    crossed = jnp.where(keep_a, b, a)
    return (
        jnp.where(keep_a, a, pltpu.roll(crossed, rolls[0], 1)),
        jnp.where(keep_a, pltpu.roll(crossed, rolls[1], 1), b),
    )


def pack(total_ref, y_lo, count, core, out_ref, out_row, halves=(0, 1)):
    group = lax.broadcasted_iota(jnp.int32, (2 * count, 128), 1) // 32
    low_half, even = group < 2, group % 2 == 0
    for half in halves:
        parts = []
        for j in range(4):
            rows = [
                total_ref[
                    pl.ds(pl.multiple_of(((2 * j + z_low) * 2 + core) * count, 8), count), half * 128 : (half + 1) * 128
                ]
                for z_low in range(2)
            ]
            parts.append(jnp.concatenate(rows, axis=0).astype(BF16))
        low_0, high_0 = exchange(parts[0], parts[2], low_half, (64, 64))
        low_1, high_1 = exchange(parts[1], parts[3], low_half, (64, 64))
        values = exchange(low_0, low_1, even, (32, 96)) + exchange(high_0, high_1, even, (32, 96))
        for dq in range(4):
            out_ref[dq * 4 + 2 * half + y_lo, out_row : out_row + 2 * count] = values[dq]


def second_kernel(
    place_ref, begun_ref, halo_ref, saved_t_ref, video_t_ref, wt_w_ref, acc_ref,
    send_ref, ws_lo_ref, ws_hi_ref, wt_lo_ref, wt_hi_ref, shifted_ref,
):
    other = 1 - place_ref[0]
    weight = [wt_w_ref[lag * C : (lag + 1) * C] for lag in range(3)]
    fill_shifted(begun_ref[0] + dot_t(halo_ref[0], weight[2]), shifted_ref, 0)
    fill_shifted(begun_ref[1] + dot_t(halo_ref[0], weight[1]) + dot_t(halo_ref[1], weight[2]), shifted_ref, 1)
    middle = acc_ref[WS + C : WS + 2 * C] + dot_n(saved_t_ref[:, 3 * PIX :], halo_ref[0])
    wt_lo_ref[:C] = acc_ref[WS : WS + C]
    wt_lo_ref[C:] = middle[: C // 2]
    wt_hi_ref[: C // 2] = middle[C // 2 :]
    wt_hi_ref[C // 2 :] = acc_ref[WS + 2 * C :] + dot_n(saved_t_ref[:, 2 * PIX :], halo_ref[...].reshape(2 * PIX, C))
    video_t = video_t_ref[:, 2 * PIX :]

    def product(tap):
        slot, low = tap_rows(tap)
        rows = shifted_ref[slot, :, low : low + PIX].reshape(2 * PIX, C)
        return acc_ref[tap * C : (tap + 1) * C] + dot_n(video_t, rows)

    for tap in range(4):
        ws_lo_ref[tap * C : (tap + 1) * C] = product(tap)
        pack((wt_lo_ref, wt_hi_ref)[tap // 2], tap // 2, 24, other, send_ref, 144, (tap % 2,))
    centre = product(4)
    ws_lo_ref[4 * C :] = centre[: C // 2]
    ws_hi_ref[: C // 2] = centre[C // 2 :]
    for tap in range(5, 9):
        low = tap * C - WS // 2
        ws_hi_ref[low : low + C] = product(tap)
        if tap < 7:
            pack(ws_lo_ref, 0, 72, other, send_ref, 0, (tap - 5,))
    pack(ws_hi_ref, 1, 72, other, send_ref, 0)


def window_kernel(
    place_ref, ws_lo_ref, ws_hi_ref, wt_lo_ref, wt_hi_ref, shifted_ref, ws_w_ref, gv_in_ref, keep_ref, gv_hbm, gv_ref, sems
):
    del gv_in_ref
    copies = []
    for frame in range(2):
        frame_gradient(shifted_ref, frame, ws_w_ref, gv_ref)
        copies.append(pltpu.make_async_copy(gv_ref.at[frame], gv_hbm.at[2 + frame], sems.at[frame]))
        copies[-1].start()
    for y_lo, (ws_ref, wt_ref) in enumerate(((ws_lo_ref, wt_lo_ref), (ws_hi_ref, wt_hi_ref))):
        pack(ws_ref, y_lo, 72, place_ref[0], keep_ref, 0)
        pack(wt_ref, y_lo, 24, place_ref[0], keep_ref, 144)
    for copy in copies:
        copy.wait()


def chip_sum_kernel(place_ref, keep_ref, other_ref, *out_refs):
    core = place_ref[0]
    for step, out_ref in enumerate(out_refs):
        for later in range(4):
            x = (place_ref[1] + jnp.where(core == 0, step, later)) & 3
            y = (place_ref[2] + jnp.where(core == 0, later, step)) & 3
            slot = x * 4 + y
            out_ref[later] = (keep_ref[slot].astype(F32) + other_ref[slot].astype(F32)).astype(BF16)


def line_sum_kernel(*refs):
    for step, out_ref in enumerate(refs[4:]):
        total = refs[0][step].astype(F32)
        for ref in refs[1:4]:
            total = total + ref[step].astype(F32)
        out_ref[...] = total.astype(BF16)


def middle_kernel(own_ref, *refs):
    out_ref, sum_ref = refs[3:]
    total = own_ref[...].astype(F32)
    for ref in refs[:3]:
        total = total + ref[...].astype(F32)
    sum_ref[...] = total
    group = lax.broadcasted_iota(jnp.int32, (24, 128), 1) // 32
    for z_low in range(2):
        rows = [sum_ref[72 * z_low + 24 * g : 72 * z_low + 24 * (g + 1)] for g in range(3)]
        rows.append(sum_ref[144 + 24 * z_low : 144 + 24 * (z_low + 1)])
        for j in range(4):
            value = rows[j]
            for g in range(4):
                if g != j:
                    value = jnp.where(group == g, pltpu.roll(rows[g], ((g - j) * 32) % 128, 1), value)
            out_ref[2 * j + z_low] = value.astype(BF16)


def last_kernel(factor, in_ref, ws_ref, wt_ref):
    total = in_ref[0].astype(F32)
    for source in range(1, 8):
        total = total + in_ref[source].astype(F32)
    total = total * factor
    for g in range(3):
        ws_ref[:, 24 * g : 24 * (g + 1)] = total[:, 32 * g : 32 * (g + 1)].T
    wt_ref[...] = total[:, 96:128]


def call(kernel, name, inputs, outputs, scratch, flops=0, moved=0, aliases=None):
    spec = {"h": pltpu.MemorySpace.HBM, "v": pltpu.MemorySpace.VMEM, "s": pltpu.MemorySpace.SMEM}
    operands = [x if space == "s" else pltpu.with_memory_space_constraint(x, spec[space]) for x, space in inputs]
    return pl.pallas_call(
        kernel,
        out_shape=[jax.ShapeDtypeStruct(shape, kind) if space == "o" else spec[space](shape, kind) for shape, kind, space in outputs],
        in_specs=[pl.BlockSpec(memory_space=spec[space]) for _, space in inputs],
        out_specs=[pl.BlockSpec() if space == "o" else pl.BlockSpec(memory_space=spec[space]) for _, _, space in outputs],
        scratch_shapes=scratch,
        input_output_aliases=aliases or {},
        compiler_params=pltpu.CompilerParams(vmem_limit_bytes=VMEM_LIMIT),
        cost_estimate=pl.CostEstimate(flops=flops, bytes_accessed=moved, transcendentals=0),
        name=name,
    )(*operands)


SLAB = (4, PIX, C)
HALF = (16, 192, 128)
ACC = (WS + WT, C)
SHIFTED = (3, 2, PIX + 2 * WID, C)


def run_first(grad, saved, video, ws_w, wt_w):
    return call(
        first_kernel,
        "first",
        [(grad, "h"), (saved, "h"), (video, "h"), (ws_w, "h"), (wt_w, "h")],
        [
            (SLAB, BF16, "h"), ((WS + WT, C), F32, "v"), ((2, PIX, C), F32, "v"), ((C, 4 * PIX), BF16, "v"), ((C, 4 * PIX), BF16, "v"),
            ((WS, C), BF16, "v"), ((WT, C), BF16, "v"),
        ],
        [
            pltpu.VMEM(SLAB, BF16),
            pltpu.VMEM(SLAB, BF16),
            pltpu.VMEM(SLAB, BF16),
            pltpu.VMEM((2, PIX, C), BF16),
            pltpu.VMEM(SHIFTED, BF16),
            pltpu.SemaphoreType.DMA((6,)),
        ],
        flops=4_000_000_000,
        moved=5_000_000,
    )


def run_second(place, begun, halo, saved_t, video_t, wt_w, acc):
    return call(
        second_kernel,
        "second",
        [(place, "s")] + [(x, "v") for x in (begun, halo, saved_t, video_t, wt_w, acc)],
        [(HALF, BF16, "v")] + [((rows // 2, C), F32, "v") for rows in (WS, WS, WT, WT)] + [(SHIFTED, BF16, "v")],
        [],
        flops=2_000_000_000,
        moved=500_000,
    )


def run_window(place, totals, shifted, ws_w, gv):
    return call(
        window_kernel,
        "window",
        [(place, "s")] + [(x, "v") for x in totals] + [(shifted, "v"), (ws_w, "v"), (gv, "h")],
        [(HALF, BF16, "v"), (SLAB, BF16, "h")],
        [pltpu.VMEM((2, PIX, C), BF16), pltpu.SemaphoreType.DMA((2,))],
        flops=1_500_000_000,
        moved=1_000_000,
        aliases={7: 1},
    )


def run_sum(kernel, name, arrays, shape, scalars=()):
    inputs = [(x, "s") for x in scalars] + [(x, "v") for x in arrays]
    return call(kernel, name, inputs, [(shape, BF16, "v")] * 4, [], moved=100_000)


def run_middle(received):
    return call(
        middle_kernel, "middle", [(x, "v") for x in received], [((8, 24, 128), BF16, "v")], [pltpu.VMEM((192, 128), F32)], moved=100_000
    )[0]


def run_last(received, factor):
    def kernel(*refs):
        last_kernel(factor, *refs)

    return call(kernel, "last", [(received, "v")], [((32, 72), F32, "o"), ((24, 32), F32, "o")], [], moved=100_000)


def ahead(step, stage):
    pairs = []
    for device in range(256):
        group, member = divmod(device, 32)
        x, y, z, core = group % 4, (group // 4) * 2 + member // 16, (member // 2) % 8, member % 2
        if core == stage:
            x = (x + step) % 4
        else:
            y = (y + step) % 4
        pairs.append((device, ((y // 2) * 4 + x) * 32 + ((y % 2) * 8 + z) * 2 + core))
    return pairs


def local(video, saved, grad_out, spatial_w, temporal_w):
    shape = grad_out.shape
    grad = grad_out.reshape(4, PIX, C)
    saved = saved.reshape(4, PIX, C)
    video = video.reshape(4, PIX, C)
    halo = lax.ppermute(grad[0:2], "frame", [(i, i - 1) for i in range(1, 32)])
    gv, acc, begun, saved_t, video_t, ws_w, wt_w = run_first(grad, saved, video, spatial_w, temporal_w)
    group, member = lax.axis_index("dp"), lax.axis_index("frame")
    place = jnp.stack([member & 1, group & 3, (group >> 2) * 2 + (member >> 4)])
    send, *totals, shifted = run_second(place, begun, halo, saved_t, video_t, wt_w, acc)
    other = lax.ppermute(send, "frame", [(i, i ^ 1) for i in range(32)])
    keep, gv = run_window(place, totals, shifted, ws_w, gv)
    parts = run_sum(chip_sum_kernel, "chip_sum", (keep, other), (4, 192, 128), (place,))
    lines = [parts[0]] + [lax.ppermute(parts[k], ("dp", "frame"), ahead(k, 0)) for k in (1, 3, 2)]
    parts = run_sum(line_sum_kernel, "line_sum", lines, (192, 128))
    planes = [parts[0]] + [lax.ppermute(parts[k], ("dp", "frame"), ahead(k, 1)) for k in (1, 3, 2)]
    blocks = run_middle(planes)
    columns = [[y * 16 + z * 2 + c for z in range(8)] for y in range(2) for c in range(2)]
    owned = lax.all_to_all(blocks, "frame", 0, 0, tiled=True, axis_index_groups=columns)
    factor = 1.0 / math.sqrt(float(8 * 128 * 8 * 64))
    grad_spatial, grad_temporal = run_last(owned, factor)
    return (gv.reshape(shape), grad_spatial.T, grad_temporal)


def solution(mesh):
    return jax.shard_map(
        local,
        mesh=mesh,
        in_specs=(
            P("dp", "frame", None, None, None),
            P("dp", "frame", None, None, None),
            P("dp", "frame", None, None, None),
            P(),
            P(),
        ),
        out_specs=(P("dp", "frame", None, None, None), P("frame", "dp"), P("frame", "dp")),
        check_vma=False,
    )
```

```python
import math

import jax
import jax.numpy as jnp
from jax import lax
from jax.experimental import pallas as pl
from jax.experimental.pallas import tpu as pltpu
from jax.sharding import PartitionSpec as P


C = 256
WID = 64
PIX = 512
WS = 9 * C
WT = 3 * C
F32 = jnp.float32
BF16 = jnp.bfloat16
VMEM_LIMIT = 24 * 1024 * 1024


def dot_t(a, b):
    return lax.dot_general(a, b, (((1,), (1,)), ((), ())), preferred_element_type=F32)


def dot_n(a, b):
    return lax.dot_general(a, b, (((1,), (0,)), ((), ())), preferred_element_type=F32)


def fill_shifted(hidden, shifted_ref, frame):
    column = lax.broadcasted_iota(jnp.int32, (PIX, C), 0) % WID
    zeros = jnp.zeros((WID, C), BF16)
    right = jnp.where(column == 0, 0.0, pltpu.roll(hidden, 1, 0))
    left = jnp.where(column == WID - 1, 0.0, pltpu.roll(hidden, PIX - 1, 0))
    for slot, value in ((0, left), (1, hidden), (2, right)):
        shifted_ref[slot, frame, 0:WID] = zeros
        shifted_ref[slot, frame, WID : WID + PIX] = value.astype(BF16)
        shifted_ref[slot, frame, WID + PIX : 2 * WID + PIX] = zeros


def tap_rows(tap):
    row_off = tap // 3 - 1
    slot = tap % 3
    return slot, WID - WID * row_off


def tap_products(shifted_ref, frames, video_t, emit):
    for tap in range(9):
        slot, low = tap_rows(tap)
        rows = shifted_ref[slot, :, low : low + PIX].reshape(frames * PIX, C)
        emit(tap, dot_n(video_t, rows))


def hidden_of(frames, wt_w_ref):
    hidden = jnp.zeros((PIX, C), F32)
    for lag in range(3):
        hidden = hidden + dot_t(frames[lag], wt_w_ref[lag * C : (lag + 1) * C])
    return hidden


def frame_gradient(shifted_ref, frame, ws_w_ref, gv_ref):
    total = jnp.zeros((PIX, C), F32)
    for tap in range(9):
        slot, low = tap_rows(tap)
        total = total + dot_t(shifted_ref[slot, frame, low : low + PIX], ws_w_ref[tap * C : (tap + 1) * C])
    gv_ref[frame] = total.astype(BF16)


def first_kernel(
    core_ref, x_ref, y_ref, grad_hbm, saved_hbm, video_hbm, ws_w_hbm, wt_w_hbm,
    gv_hbm, acc_ref, begun_ref, saved_t_ref, video_t_ref, ws_w_ref, wt_w_ref,
    grad_ref, saved_ref, video_ref, gv_ref, shifted_ref, sems,
):
    del core_ref, x_ref, y_ref
    sources = (saved_hbm, grad_hbm, wt_w_hbm, video_hbm, ws_w_hbm)
    targets = (saved_ref, grad_ref, wt_w_ref, video_ref, ws_w_ref)
    copies = [pltpu.make_async_copy(a, b, sems.at[i]) for i, (a, b) in enumerate(zip(sources, targets))]
    for copy in copies:
        copy.start()
    copies[0].wait()
    for frame in range(4):
        saved_t_ref[:, frame * PIX : (frame + 1) * PIX] = saved_ref[frame].T
    copies[1].wait()
    for lag in range(3):
        rows = grad_ref[lag:4].reshape((4 - lag) * PIX, C)
        acc_ref[WS + lag * C : WS + (lag + 1) * C] = dot_n(saved_t_ref[:, : (4 - lag) * PIX], rows)
    copies[2].wait()
    for frame in range(2):
        fill_shifted(hidden_of([grad_ref[frame + lag] for lag in range(3)], wt_w_ref), shifted_ref, frame)
    copies[3].wait()
    for frame in range(4):
        video_t_ref[:, frame * PIX : (frame + 1) * PIX] = video_ref[frame].T
    copies[4].wait()
    for frame in range(2):
        frame_gradient(shifted_ref, frame, ws_w_ref, gv_ref)
    out = pltpu.make_async_copy(gv_ref, gv_hbm.at[0:2], sems.at[5])
    out.start()

    def emit(tap, value):
        acc_ref[tap * C : (tap + 1) * C] = value

    tap_products(shifted_ref, 2, video_t_ref[:, : 2 * PIX], emit)
    weight = [wt_w_ref[lag * C : (lag + 1) * C] for lag in range(2)]
    begun_ref[0] = dot_t(grad_ref[2], weight[0]) + dot_t(grad_ref[3], weight[1])
    begun_ref[1] = dot_t(grad_ref[3], weight[0])
    out.wait()


def exchange(a, b, keep_a, rolls):
    crossed = jnp.where(keep_a, b, a)
    return (
        jnp.where(keep_a, a, pltpu.roll(crossed, rolls[0], 1)),
        jnp.where(keep_a, pltpu.roll(crossed, rolls[1], 1), b),
    )


def pack(total_ref, y_lo, count, core, out_ref, out_row, halves=(0, 1)):
    group = lax.broadcasted_iota(jnp.int32, (2 * count, 128), 1) // 32
    low_half, even = group < 2, group % 2 == 0
    for half in halves:
        parts = []
        for j in range(4):
            rows = [
                total_ref[
                    pl.ds(pl.multiple_of(((2 * j + z_low) * 2 + core) * count, 8), count), half * 128 : (half + 1) * 128
                ]
                for z_low in range(2)
            ]
            parts.append(jnp.concatenate(rows, axis=0).astype(BF16))
        low_0, high_0 = exchange(parts[0], parts[2], low_half, (64, 64))
        low_1, high_1 = exchange(parts[1], parts[3], low_half, (64, 64))
        values = exchange(low_0, low_1, even, (32, 96)) + exchange(high_0, high_1, even, (32, 96))
        for dq in range(4):
            out_ref[dq * 4 + 2 * half + y_lo, out_row : out_row + 2 * count] = values[dq]


def second_kernel(
    core_ref, begun_ref, halo_ref, saved_t_ref, video_t_ref, wt_w_ref, acc_ref,
    send_ref, ws_lo_ref, ws_hi_ref, wt_lo_ref, wt_hi_ref, shifted_ref,
):
    other = 1 - core_ref[0]
    weight = [wt_w_ref[lag * C : (lag + 1) * C] for lag in range(3)]
    fill_shifted(begun_ref[0] + dot_t(halo_ref[0], weight[2]), shifted_ref, 0)
    fill_shifted(begun_ref[1] + dot_t(halo_ref[0], weight[1]) + dot_t(halo_ref[1], weight[2]), shifted_ref, 1)
    middle = acc_ref[WS + C : WS + 2 * C] + dot_n(saved_t_ref[:, 3 * PIX :], halo_ref[0])
    wt_lo_ref[:C] = acc_ref[WS : WS + C]
    wt_lo_ref[C:] = middle[: C // 2]
    wt_hi_ref[: C // 2] = middle[C // 2 :]
    wt_hi_ref[C // 2 :] = acc_ref[WS + 2 * C :] + dot_n(saved_t_ref[:, 2 * PIX :], halo_ref[...].reshape(2 * PIX, C))
    video_t = video_t_ref[:, 2 * PIX :]

    def product(tap):
        slot, low = tap_rows(tap)
        rows = shifted_ref[slot, :, low : low + PIX].reshape(2 * PIX, C)
        return acc_ref[tap * C : (tap + 1) * C] + dot_n(video_t, rows)

    for tap in range(4):
        ws_lo_ref[tap * C : (tap + 1) * C] = product(tap)
        pack((wt_lo_ref, wt_hi_ref)[tap // 2], tap // 2, 24, other, send_ref, 144, (tap % 2,))
    centre = product(4)
    ws_lo_ref[4 * C :] = centre[: C // 2]
    ws_hi_ref[: C // 2] = centre[C // 2 :]
    for tap in range(5, 9):
        low = tap * C - WS // 2
        ws_hi_ref[low : low + C] = product(tap)
        if tap < 7:
            pack(ws_lo_ref, 0, 72, other, send_ref, 0, (tap - 5,))
    pack(ws_hi_ref, 1, 72, other, send_ref, 0)


def window_kernel(
    core_ref, ws_lo_ref, ws_hi_ref, wt_lo_ref, wt_hi_ref, shifted_ref, ws_w_ref, gv_in_ref, keep_ref, gv_hbm, gv_ref, sems
):
    del gv_in_ref
    copies = []
    for frame in range(2):
        frame_gradient(shifted_ref, frame, ws_w_ref, gv_ref)
        copies.append(pltpu.make_async_copy(gv_ref.at[frame], gv_hbm.at[2 + frame], sems.at[frame]))
        copies[-1].start()
    for y_lo, (ws_ref, wt_ref) in enumerate(((ws_lo_ref, wt_lo_ref), (ws_hi_ref, wt_hi_ref))):
        pack(ws_ref, y_lo, 72, core_ref[0], keep_ref, 0)
        pack(wt_ref, y_lo, 24, core_ref[0], keep_ref, 144)
    for copy in copies:
        copy.wait()


def chip_sum_kernel(core_ref, x_ref, y_ref, keep_ref, other_ref, *out_refs):
    core = core_ref[0]
    for step, out_ref in enumerate(out_refs):
        for later in range(4):
            x = (x_ref[0] + jnp.where(core == 0, step, later)) & 3
            y = (y_ref[0] + jnp.where(core == 0, later, step)) & 3
            slot = x * 4 + y
            out_ref[later] = (keep_ref[slot].astype(F32) + other_ref[slot].astype(F32)).astype(BF16)


def line_sum_kernel(*refs):
    for step, out_ref in enumerate(refs[4:]):
        total = refs[0][step].astype(F32)
        for ref in refs[1:4]:
            total = total + ref[step].astype(F32)
        out_ref[...] = total.astype(BF16)


def middle_kernel(own_ref, *refs):
    out_ref, sum_ref = refs[3:]
    total = own_ref[...].astype(F32)
    for ref in refs[:3]:
        total = total + ref[...].astype(F32)
    sum_ref[...] = total
    group = lax.broadcasted_iota(jnp.int32, (24, 128), 1) // 32
    for z_low in range(2):
        rows = [sum_ref[72 * z_low + 24 * g : 72 * z_low + 24 * (g + 1)] for g in range(3)]
        rows.append(sum_ref[144 + 24 * z_low : 144 + 24 * (z_low + 1)])
        for j in range(4):
            value = rows[j]
            for g in range(4):
                if g != j:
                    value = jnp.where(group == g, pltpu.roll(rows[g], ((g - j) * 32) % 128, 1), value)
            out_ref[2 * j + z_low] = value.astype(BF16)


def last_kernel(factor, in_ref, ws_ref, wt_ref):
    total = in_ref[0].astype(F32)
    for source in range(1, 8):
        total = total + in_ref[source].astype(F32)
    total = total * factor
    for g in range(3):
        ws_ref[:, 24 * g : 24 * (g + 1)] = total[:, 32 * g : 32 * (g + 1)].T
    wt_ref[...] = total[:, 96:128]


def call(kernel, name, inputs, outputs, scratch, flops=0, moved=0, aliases=None):
    spec = {"h": pltpu.MemorySpace.HBM, "v": pltpu.MemorySpace.VMEM, "s": pltpu.MemorySpace.SMEM}
    operands = [x if space == "s" else pltpu.with_memory_space_constraint(x, spec[space]) for x, space in inputs]
    return pl.pallas_call(
        kernel,
        out_shape=[jax.ShapeDtypeStruct(shape, kind) if space == "o" else spec[space](shape, kind) for shape, kind, space in outputs],
        in_specs=[pl.BlockSpec(memory_space=spec[space]) for _, space in inputs],
        out_specs=[pl.BlockSpec() if space == "o" else pl.BlockSpec(memory_space=spec[space]) for _, _, space in outputs],
        scratch_shapes=scratch,
        input_output_aliases=aliases or {},
        compiler_params=pltpu.CompilerParams(vmem_limit_bytes=VMEM_LIMIT),
        cost_estimate=pl.CostEstimate(flops=flops, bytes_accessed=moved, transcendentals=0),
        name=name,
    )(*operands)


SLAB = (4, PIX, C)
HALF = (16, 192, 128)
ACC = (WS + WT, C)
SHIFTED = (3, 2, PIX + 2 * WID, C)


def run_first(scalars, grad, saved, video, ws_w, wt_w):
    return call(
        first_kernel,
        "first",
        [(x, "s") for x in scalars] + [(x, "h") for x in (grad, saved, video, ws_w, wt_w)],
        [
            (SLAB, BF16, "h"), ((WS + WT, C), F32, "v"), ((2, PIX, C), F32, "v"), ((C, 4 * PIX), BF16, "v"), ((C, 4 * PIX), BF16, "v"),
            ((WS, C), BF16, "v"), ((WT, C), BF16, "v"),
        ],
        [
            pltpu.VMEM(SLAB, BF16),
            pltpu.VMEM(SLAB, BF16),
            pltpu.VMEM(SLAB, BF16),
            pltpu.VMEM((2, PIX, C), BF16),
            pltpu.VMEM(SHIFTED, BF16),
            pltpu.SemaphoreType.DMA((6,)),
        ],
        flops=4_000_000_000,
        moved=5_000_000,
    )


def run_second(core, begun, halo, saved_t, video_t, wt_w, acc):
    return call(
        second_kernel,
        "second",
        [(core, "s")] + [(x, "v") for x in (begun, halo, saved_t, video_t, wt_w, acc)],
        [(HALF, BF16, "v")] + [((rows // 2, C), F32, "v") for rows in (WS, WS, WT, WT)] + [(SHIFTED, BF16, "v")],
        [],
        flops=2_000_000_000,
        moved=500_000,
    )


def run_window(core, totals, shifted, ws_w, gv):
    return call(
        window_kernel,
        "window",
        [(core, "s")] + [(x, "v") for x in totals] + [(shifted, "v"), (ws_w, "v"), (gv, "h")],
        [(HALF, BF16, "v"), (SLAB, BF16, "h")],
        [pltpu.VMEM((2, PIX, C), BF16), pltpu.SemaphoreType.DMA((2,))],
        flops=1_500_000_000,
        moved=1_000_000,
        aliases={7: 1},
    )


def run_sum(kernel, name, arrays, shape, scalars=()):
    inputs = [(x, "s") for x in scalars] + [(x, "v") for x in arrays]
    return call(kernel, name, inputs, [(shape, BF16, "v")] * 4, [], moved=100_000)


def run_middle(received):
    return call(
        middle_kernel, "middle", [(x, "v") for x in received], [((8, 24, 128), BF16, "v")], [pltpu.VMEM((192, 128), F32)], moved=100_000
    )[0]


def run_last(received, factor):
    def kernel(*refs):
        last_kernel(factor, *refs)

    return call(kernel, "last", [(received, "v")], [((32, 72), F32, "o"), ((24, 32), F32, "o")], [], moved=100_000)


def ahead(step, stage):
    pairs = []
    for device in range(256):
        group, member = divmod(device, 32)
        x, y, z, core = group % 4, (group // 4) * 2 + member // 16, (member // 2) % 8, member % 2
        if core == stage:
            x = (x + step) % 4
        else:
            y = (y + step) % 4
        pairs.append((device, ((y // 2) * 4 + x) * 32 + ((y % 2) * 8 + z) * 2 + core))
    return pairs


def local(video, saved, grad_out, spatial_w, temporal_w):
    shape = grad_out.shape
    grad = grad_out.reshape(4, PIX, C)
    saved = saved.reshape(4, PIX, C)
    video = video.reshape(4, PIX, C)
    halo = lax.ppermute(grad[0:2], "frame", [(i, i - 1) for i in range(1, 32)])
    group, member = lax.axis_index("dp"), lax.axis_index("frame")
    core, x, y = (v.reshape(1) for v in (member & 1, group & 3, ((group >> 2) << 1) | (member >> 4)))
    gv, acc, begun, saved_t, video_t, ws_w, wt_w = run_first((core, x, y), grad, saved, video, spatial_w, temporal_w)
    send, *totals, shifted = run_second(core, begun, halo, saved_t, video_t, wt_w, acc)
    other = lax.ppermute(send, "frame", [(i, i ^ 1) for i in range(32)])
    keep, gv = run_window(core, totals, shifted, ws_w, gv)
    parts = run_sum(chip_sum_kernel, "chip_sum", (keep, other), (4, 192, 128), (core, x, y))
    lines = [parts[0]] + [lax.ppermute(parts[k], ("dp", "frame"), ahead(k, 0)) for k in (1, 3, 2)]
    parts = run_sum(line_sum_kernel, "line_sum", lines, (192, 128))
    planes = [parts[0]] + [lax.ppermute(parts[k], ("dp", "frame"), ahead(k, 1)) for k in (1, 3, 2)]
    blocks = run_middle(planes)
    columns = [[y * 16 + z * 2 + c for z in range(8)] for y in range(2) for c in range(2)]
    owned = lax.all_to_all(blocks, "frame", 0, 0, tiled=True, axis_index_groups=columns)
    factor = 1.0 / math.sqrt(float(8 * 128 * 8 * 64))
    grad_spatial, grad_temporal = run_last(owned, factor)
    return (gv.reshape(shape), grad_spatial.T, grad_temporal)


def solution(mesh):
    return jax.shard_map(
        local,
        mesh=mesh,
        in_specs=(
            P("dp", "frame", None, None, None),
            P("dp", "frame", None, None, None),
            P("dp", "frame", None, None, None),
            P(),
            P(),
        ),
        out_specs=(P("dp", "frame", None, None, None), P("frame", "dp"), P("frame", "dp")),
        check_vma=False,
    )
```

```python
import math

import jax
import jax.numpy as jnp
from jax import lax
from jax.experimental import pallas as pl
from jax.experimental.pallas import tpu as pltpu
from jax.sharding import PartitionSpec as P


C = 256
WID = 64
PIX = 512
WS = 9 * C
WT = 3 * C
F32 = jnp.float32
BF16 = jnp.bfloat16
VMEM_LIMIT = 24 * 1024 * 1024


def dot_t(a, b):
    return lax.dot_general(a, b, (((1,), (1,)), ((), ())), preferred_element_type=F32)


def dot_n(a, b):
    return lax.dot_general(a, b, (((1,), (0,)), ((), ())), preferred_element_type=F32)


def fill_shifted(hidden, shifted_ref, frame):
    column = lax.broadcasted_iota(jnp.int32, (PIX, C), 0) % WID
    zeros = jnp.zeros((WID, C), BF16)
    right = jnp.where(column == 0, 0.0, pltpu.roll(hidden, 1, 0))
    left = jnp.where(column == WID - 1, 0.0, pltpu.roll(hidden, PIX - 1, 0))
    for slot, value in ((0, left), (1, hidden), (2, right)):
        shifted_ref[slot, frame, 0:WID] = zeros
        shifted_ref[slot, frame, WID : WID + PIX] = value.astype(BF16)
        shifted_ref[slot, frame, WID + PIX : 2 * WID + PIX] = zeros


def tap_rows(tap):
    row_off = tap // 3 - 1
    slot = tap % 3
    return slot, WID - WID * row_off


def tap_products(shifted_ref, frames, video_t, emit):
    for tap in range(9):
        slot, low = tap_rows(tap)
        rows = shifted_ref[slot, :, low : low + PIX].reshape(frames * PIX, C)
        emit(tap, dot_n(video_t, rows))


def hidden_of(frames, wt_w_ref):
    hidden = jnp.zeros((PIX, C), F32)
    for lag in range(3):
        hidden = hidden + dot_t(frames[lag], wt_w_ref[lag * C : (lag + 1) * C])
    return hidden


def frame_gradient(shifted_ref, frame, ws_w_ref, gv_ref):
    total = jnp.zeros((PIX, C), F32)
    for tap in range(9):
        slot, low = tap_rows(tap)
        total = total + dot_t(shifted_ref[slot, frame, low : low + PIX], ws_w_ref[tap * C : (tap + 1) * C])
    gv_ref[frame] = total.astype(BF16)


def first_kernel(
    core_ref, x_ref, y_ref, grad_hbm, saved_hbm, video_hbm, ws_w_hbm, wt_w_hbm,
    gv_hbm, acc_ref, begun_ref, saved_t_ref, video_t_ref, ws_w_ref, wt_w_ref,
    grad_ref, saved_ref, video_ref, gv_ref, shifted_ref, sems,
):
    del core_ref, x_ref, y_ref
    sources = (saved_hbm, grad_hbm, wt_w_hbm, video_hbm, ws_w_hbm)
    targets = (saved_ref, grad_ref, wt_w_ref, video_ref, ws_w_ref)
    copies = [pltpu.make_async_copy(a, b, sems.at[i]) for i, (a, b) in enumerate(zip(sources, targets))]
    for copy in copies:
        copy.start()
    copies[0].wait()
    for frame in range(4):
        saved_t_ref[:, frame * PIX : (frame + 1) * PIX] = saved_ref[frame].T
    copies[1].wait()
    for lag in range(3):
        rows = grad_ref[lag:4].reshape((4 - lag) * PIX, C)
        acc_ref[WS + lag * C : WS + (lag + 1) * C] = dot_n(saved_t_ref[:, : (4 - lag) * PIX], rows)
    copies[2].wait()
    for frame in range(2):
        fill_shifted(hidden_of([grad_ref[frame + lag] for lag in range(3)], wt_w_ref), shifted_ref, frame)
    copies[3].wait()
    for frame in range(4):
        video_t_ref[:, frame * PIX : (frame + 1) * PIX] = video_ref[frame].T
    copies[4].wait()
    for frame in range(2):
        frame_gradient(shifted_ref, frame, ws_w_ref, gv_ref)
    out = pltpu.make_async_copy(gv_ref, gv_hbm.at[0:2], sems.at[5])
    out.start()

    def emit(tap, value):
        acc_ref[tap * C : (tap + 1) * C] = value

    tap_products(shifted_ref, 2, video_t_ref[:, : 2 * PIX], emit)
    weight = [wt_w_ref[lag * C : (lag + 1) * C] for lag in range(2)]
    begun_ref[0] = dot_t(grad_ref[2], weight[0]) + dot_t(grad_ref[3], weight[1])
    begun_ref[1] = dot_t(grad_ref[3], weight[0])
    out.wait()


def exchange(a, b, keep_a, rolls):
    crossed = jnp.where(keep_a, b, a)
    return (
        jnp.where(keep_a, a, pltpu.roll(crossed, rolls[0], 1)),
        jnp.where(keep_a, pltpu.roll(crossed, rolls[1], 1), b),
    )


def pack(total_ref, y_lo, count, core, out_ref, out_row, halves=(0, 1)):
    group = lax.broadcasted_iota(jnp.int32, (2 * count, 128), 1) // 32
    low_half, even = group < 2, group % 2 == 0
    for half in halves:
        parts = []
        for j in range(4):
            rows = [
                total_ref[
                    pl.ds(pl.multiple_of(((2 * j + z_low) * 2 + core) * count, 8), count), half * 128 : (half + 1) * 128
                ]
                for z_low in range(2)
            ]
            parts.append(jnp.concatenate(rows, axis=0).astype(BF16))
        low_0, high_0 = exchange(parts[0], parts[2], low_half, (64, 64))
        low_1, high_1 = exchange(parts[1], parts[3], low_half, (64, 64))
        values = exchange(low_0, low_1, even, (32, 96)) + exchange(high_0, high_1, even, (32, 96))
        for dq in range(4):
            out_ref[dq * 4 + 2 * half + y_lo, out_row : out_row + 2 * count] = values[dq]


def second_kernel(
    core_ref, begun_ref, halo_ref, saved_t_ref, video_t_ref, wt_w_ref, acc_ref,
    send_ref, ws_lo_ref, ws_hi_ref, wt_lo_ref, wt_hi_ref, shifted_ref,
):
    other = 1 - core_ref[0]
    weight = [wt_w_ref[lag * C : (lag + 1) * C] for lag in range(3)]
    fill_shifted(begun_ref[0] + dot_t(halo_ref[0], weight[2]), shifted_ref, 0)
    fill_shifted(begun_ref[1] + dot_t(halo_ref[0], weight[1]) + dot_t(halo_ref[1], weight[2]), shifted_ref, 1)
    middle = acc_ref[WS + C : WS + 2 * C] + dot_n(saved_t_ref[:, 3 * PIX :], halo_ref[0])
    wt_lo_ref[:C] = acc_ref[WS : WS + C]
    wt_lo_ref[C:] = middle[: C // 2]
    wt_hi_ref[: C // 2] = middle[C // 2 :]
    wt_hi_ref[C // 2 :] = acc_ref[WS + 2 * C :] + dot_n(saved_t_ref[:, 2 * PIX :], halo_ref[...].reshape(2 * PIX, C))
    video_t = video_t_ref[:, 2 * PIX :]

    def product(tap):
        slot, low = tap_rows(tap)
        rows = shifted_ref[slot, :, low : low + PIX].reshape(2 * PIX, C)
        return acc_ref[tap * C : (tap + 1) * C] + dot_n(video_t, rows)

    for tap in range(4):
        ws_lo_ref[tap * C : (tap + 1) * C] = product(tap)
        pack((wt_lo_ref, wt_hi_ref)[tap // 2], tap // 2, 24, other, send_ref, 144, (tap % 2,))
    centre = product(4)
    ws_lo_ref[4 * C :] = centre[: C // 2]
    ws_hi_ref[: C // 2] = centre[C // 2 :]
    for tap in range(5, 9):
        low = tap * C - WS // 2
        ws_hi_ref[low : low + C] = product(tap)
        if tap < 7:
            pack(ws_lo_ref, 0, 72, other, send_ref, 0, (tap - 5,))
    pack(ws_hi_ref, 1, 72, other, send_ref, 0)


def window_kernel(
    core_ref, ws_lo_ref, ws_hi_ref, wt_lo_ref, wt_hi_ref, shifted_ref, ws_w_ref, gv_in_ref, keep_ref, gv_hbm, gv_ref, sems
):
    del gv_in_ref
    copies = []
    for frame in range(2):
        frame_gradient(shifted_ref, frame, ws_w_ref, gv_ref)
        copies.append(pltpu.make_async_copy(gv_ref.at[frame], gv_hbm.at[2 + frame], sems.at[frame]))
        copies[-1].start()
    for y_lo, (ws_ref, wt_ref) in enumerate(((ws_lo_ref, wt_lo_ref), (ws_hi_ref, wt_hi_ref))):
        pack(ws_ref, y_lo, 72, core_ref[0], keep_ref, 0)
        pack(wt_ref, y_lo, 24, core_ref[0], keep_ref, 144)
    for copy in copies:
        copy.wait()


def chip_sum_kernel(core_ref, x_ref, y_ref, keep_ref, other_ref, *out_refs):
    core = core_ref[0]
    for step, out_ref in enumerate(out_refs):
        for later in range(4):
            x = (x_ref[0] + jnp.where(core == 0, step, later)) & 3
            y = (y_ref[0] + jnp.where(core == 0, later, step)) & 3
            slot = x * 4 + y
            out_ref[later] = (keep_ref[slot].astype(F32) + other_ref[slot].astype(F32)).astype(BF16)


def line_sum_kernel(*refs):
    for step, out_ref in enumerate(refs[4:]):
        total = refs[0][step].astype(F32)
        for ref in refs[1:4]:
            total = total + ref[step].astype(F32)
        out_ref[...] = total.astype(BF16)


def middle_kernel(own_ref, *refs):
    out_ref, sum_ref = refs[3:]
    total = own_ref[...].astype(F32)
    for ref in refs[:3]:
        total = total + ref[...].astype(F32)
    sum_ref[...] = total
    group = lax.broadcasted_iota(jnp.int32, (24, 128), 1) // 32
    for z_low in range(2):
        rows = [sum_ref[72 * z_low + 24 * g : 72 * z_low + 24 * (g + 1)] for g in range(3)]
        rows.append(sum_ref[144 + 24 * z_low : 144 + 24 * (z_low + 1)])
        for j in range(4):
            value = rows[j]
            for g in range(4):
                if g != j:
                    value = jnp.where(group == g, pltpu.roll(rows[g], ((g - j) * 32) % 128, 1), value)
            out_ref[2 * j + z_low] = value.astype(BF16)


def last_kernel(factor, in_ref, ws_ref, wt_ref):
    total = in_ref[0].astype(F32)
    for source in range(1, 8):
        total = total + in_ref[source].astype(F32)
    total = total * factor
    for g in range(3):
        ws_ref[:, 24 * g : 24 * (g + 1)] = total[:, 32 * g : 32 * (g + 1)].T
    wt_ref[...] = total[:, 96:128]


def call(kernel, name, inputs, outputs, scratch, flops=0, moved=0, aliases=None):
    spec = {"h": pltpu.MemorySpace.HBM, "v": pltpu.MemorySpace.VMEM, "s": pltpu.MemorySpace.SMEM}
    operands = [x if space == "s" else pltpu.with_memory_space_constraint(x, spec[space]) for x, space in inputs]
    return pl.pallas_call(
        kernel,
        out_shape=[jax.ShapeDtypeStruct(shape, kind) if space == "o" else spec[space](shape, kind) for shape, kind, space in outputs],
        in_specs=[pl.BlockSpec(memory_space=spec[space]) for _, space in inputs],
        out_specs=[pl.BlockSpec() if space == "o" else pl.BlockSpec(memory_space=spec[space]) for _, _, space in outputs],
        scratch_shapes=scratch,
        input_output_aliases=aliases or {},
        compiler_params=pltpu.CompilerParams(vmem_limit_bytes=VMEM_LIMIT),
        cost_estimate=pl.CostEstimate(flops=flops, bytes_accessed=moved, transcendentals=0),
        name=name,
    )(*operands)


SLAB = (4, PIX, C)
HALF = (16, 192, 128)
ACC = (WS + WT, C)
SHIFTED = (3, 2, PIX + 2 * WID, C)


def run_first(scalars, grad, saved, video, ws_w, wt_w):
    return call(
        first_kernel,
        "first",
        [(x, "s") for x in scalars] + [(x, "h") for x in (grad, saved, video, ws_w, wt_w)],
        [
            (SLAB, BF16, "h"), ((WS + WT, C), F32, "v"), ((2, PIX, C), F32, "v"), ((C, 4 * PIX), BF16, "v"), ((C, 4 * PIX), BF16, "v"),
            ((WS, C), BF16, "v"), ((WT, C), BF16, "v"),
        ],
        [
            pltpu.VMEM(SLAB, BF16),
            pltpu.VMEM(SLAB, BF16),
            pltpu.VMEM(SLAB, BF16),
            pltpu.VMEM((2, PIX, C), BF16),
            pltpu.VMEM(SHIFTED, BF16),
            pltpu.SemaphoreType.DMA((6,)),
        ],
        flops=4_000_000_000,
        moved=5_000_000,
    )


def run_second(core, begun, halo, saved_t, video_t, wt_w, acc):
    return call(
        second_kernel,
        "second",
        [(core, "s")] + [(x, "v") for x in (begun, halo, saved_t, video_t, wt_w, acc)],
        [(HALF, BF16, "v")] + [((rows // 2, C), F32, "v") for rows in (WS, WS, WT, WT)] + [(SHIFTED, BF16, "v")],
        [],
        flops=2_000_000_000,
        moved=500_000,
    )


def run_window(core, totals, shifted, ws_w, gv):
    return call(
        window_kernel,
        "window",
        [(core, "s")] + [(x, "v") for x in totals] + [(shifted, "v"), (ws_w, "v"), (gv, "h")],
        [(HALF, BF16, "v"), (SLAB, BF16, "h")],
        [pltpu.VMEM((2, PIX, C), BF16), pltpu.SemaphoreType.DMA((2,))],
        flops=1_500_000_000,
        moved=1_000_000,
        aliases={7: 1},
    )


def run_sum(kernel, name, arrays, shape, scalars=()):
    inputs = [(x, "s") for x in scalars] + [(x, "v") for x in arrays]
    return call(kernel, name, inputs, [(shape, BF16, "v")] * 4, [], moved=100_000)


def run_middle(received):
    return call(
        middle_kernel, "middle", [(x, "v") for x in received], [((8, 24, 128), BF16, "v")], [pltpu.VMEM((192, 128), F32)], moved=100_000
    )[0]


def run_last(received, factor):
    def kernel(*refs):
        last_kernel(factor, *refs)

    return call(kernel, "last", [(received, "v")], [((32, 72), F32, "o"), ((24, 32), F32, "o")], [], moved=100_000)


def ahead(step, stage):
    pairs = []
    for device in range(256):
        group, member = divmod(device, 32)
        x, y, z, core = group % 4, (group // 4) * 2 + member // 16, (member // 2) % 8, member % 2
        if core == stage:
            x = (x + step) % 4
        else:
            y = (y + step) % 4
        pairs.append((device, ((y // 2) * 4 + x) * 32 + ((y % 2) * 8 + z) * 2 + core))
    return pairs


def local(video, saved, grad_out, spatial_w, temporal_w):
    shape = grad_out.shape
    grad = grad_out.reshape(4, PIX, C)
    saved = saved.reshape(4, PIX, C)
    video = video.reshape(4, PIX, C)
    halo = lax.ppermute(grad[0:2], "frame", [(i, i - 1) for i in range(1, 32)])
    group, member = lax.axis_index("dp"), lax.axis_index("frame")
    core, x, y = (v.reshape(1) for v in (member & 1, group & 3, ((group >> 2) << 1) | (member >> 4)))
    gv, acc, begun, saved_t, video_t, ws_w, wt_w = run_first((core, x, y), grad, saved, video, spatial_w, temporal_w)
    send, *totals, shifted = run_second(core, begun, halo, saved_t, video_t, wt_w, acc)
    other = lax.ppermute(send, "frame", [(i, i ^ 1) for i in range(32)])
    keep, gv = run_window(core, totals, shifted, ws_w, gv)
    parts = run_sum(chip_sum_kernel, "chip_sum", (keep, other), (4, 192, 128), (core, x, y))
    lines = [parts[0]] + [lax.ppermute(parts[k], ("dp", "frame"), ahead(k, 0)) for k in (2, 1, 3)]
    parts = run_sum(line_sum_kernel, "line_sum", lines, (192, 128))
    planes = [parts[0]] + [lax.ppermute(parts[k], ("dp", "frame"), ahead(k, 1)) for k in (2, 1, 3)]
    blocks = run_middle(planes)
    columns = [[y * 16 + z * 2 + c for z in range(8)] for y in range(2) for c in range(2)]
    owned = lax.all_to_all(blocks, "frame", 0, 0, tiled=True, axis_index_groups=columns)
    factor = 1.0 / math.sqrt(float(8 * 128 * 8 * 64))
    grad_spatial, grad_temporal = run_last(owned, factor)
    return (gv.reshape(shape), grad_spatial.T, grad_temporal)


def solution(mesh):
    return jax.shard_map(
        local,
        mesh=mesh,
        in_specs=(
            P("dp", "frame", None, None, None),
            P("dp", "frame", None, None, None),
            P("dp", "frame", None, None, None),
            P(),
            P(),
        ),
        out_specs=(P("dp", "frame", None, None, None), P("frame", "dp"), P("frame", "dp")),
        check_vma=False,
    )
```
